256 devices in a mesh: gx: 4 (over z_lo, core), gy: 16 (over x, z_hi), gz: 4 (over y).
Axes of the slice: x: 4, y: 4, z: 8 (z_hi: 4, z_lo: 2; z = z_hi * 2 + z_lo), core: 2. Of those that a mesh axis runs over, the one named last changes fastest.
Arguments:
- displacement: float32 [3, 32, 512, 1024], P(None, 'gx', 'gy', 'gz'), may hold values from -1.5 to 1.5
- velocity: float32 [3, 32, 512, 1024], P(None, 'gx', 'gy', 'gz'), may hold values from -6 to 6
- density: float32 [16, 256, 512], P('gx', 'gy', 'gz'), may hold values from 0.5 to 2
- energy: float32 [16, 256, 512], P('gx', 'gy', 'gz'), may hold values from 0.2 to 24
- region: int32 [16, 256, 512], P('gx', 'gy', 'gz'), may hold values from 0 to 3
- heat_ratio: float32 [4], replicated, may hold values from 1.3 to 3
- tracer: float32 [16, 256, 512], P('gx', 'gy', 'gz'), may hold values from -6 to 6
Outputs:
- new_velocity: float32 [3, 32, 512, 1024], P(None, 'gx', 'gy', 'gz')
- relaxed_mesh: float32 [3, 32, 512, 1024], P(None, 'gx', 'gy', 'gz')
- remapped: float32 [16, 256, 512], P('gx', 'gy', 'gz')
The draws below stay inside these ranges and needn't reach their ends.
All inputs are finite; a program needn't handle non-finite values.
Results may differ from the reference program's by a relative error of at most 0.00002.
Values sent between devices are 32-bit elements; how exact they have to be, the bound alone decides.
No kernel may reach another device: no remote copies, remote signals or barrier semaphores. Data moves between devices by JAX's collectives and lax.ppermute only.
A program may use at most 64 MiB of HBM per device.

```python
import math
import jax
import jax.numpy as jnp
from jax import lax

ZX = 4
ZY = 16
ZZ = 128
REGIONS = 4
NZX = 16
NZY = 256
NZZ = 512


def draw_energy(key, part):
    tile_key = jax.random.fold_in(key, 11)
    zone_key = jax.random.fold_in(key, 12)
    tile_draw = jax.random.uniform(tile_key, (NZX // ZX, NZY // ZY, NZZ // ZZ), jnp.float32)
    factor = jnp.exp(tile_draw * jnp.log(16.0))
    factor = jnp.repeat(jnp.repeat(jnp.repeat(factor, ZX, 0), ZY, 1), ZZ, 2)
    zone_draw = jax.random.uniform(zone_key, (NZX, NZY, NZZ), jnp.float32, 0.5, 1.5)
    return (zone_draw * factor).astype(jnp.float32)


def place_ends(array, rng, least, top_value):
    spot = [jax.random.randint(jax.random.fold_in(rng, axis), (), 0, length) for axis, length in enumerate(array.shape)]
    main_axis = array.shape.index(max(array.shape))
    neighbour = spot[:main_axis] + [(spot[main_axis] + 1) % array.shape[main_axis]] + spot[main_axis + 1:]
    return array.at[tuple(spot)].set(least).at[tuple(neighbour)].set(top_value)


def shard_levels(key, dims, shards, low, largest):
    level = 1.0
    for axis_at, blocks in shards:
        heights = jax.random.uniform(jax.random.fold_in(jax.random.fold_in(key, 6), axis_at), (blocks,), jnp.float32, low / len(shards), largest / len(shards))
        level = level * jnp.repeat(jnp.exp(heights), dims[axis_at] // blocks).reshape((-1,) + (1,) * (len(dims) - 1 - axis_at))
    return level


def gaussian(own_key, dims, spread, bound, cuts=(), kind=jnp.bfloat16):
    values = spread * jax.random.normal(own_key, dims, jnp.float32)
    if cuts:
        values = values * shard_levels(own_key, dims, cuts, -0.22, 0.18)
    return jnp.clip(values, -bound, bound).astype(kind)


def setup_inputs(seed: int = 0) -> dict:
    arg_keys = jax.random.split(jax.random.key(seed), 8)
    return {
        "displacement": gaussian(arg_keys[0], (3, 2 * NZX, 2 * NZY, 2 * NZZ), 0.25, 1.5, ((1, 4), (2, 16), (3, 4)), jnp.float32),
        "velocity": gaussian(arg_keys[1], (3, 2 * NZX, 2 * NZY, 2 * NZZ), 1.0, 6.0, ((1, 4), (2, 16), (3, 4)), jnp.float32),
        "density": jnp.clip(jnp.exp(math.log(2.0) - 1.3862944 * jax.random.uniform(arg_keys[2], (NZX, NZY, NZZ), jnp.float32) ** shard_levels(arg_keys[2], (NZX, NZY, NZZ), ((0, 4), (1, 16), (2, 4)), -0.2, 0.2)), 0.5, 2.0),
        "energy": draw_energy(jax.random.fold_in(arg_keys[7], 71), 0),
        "region": place_ends(jax.random.randint(arg_keys[4], (NZX, NZY, NZZ), 0, REGIONS), jax.random.fold_in(arg_keys[4], 1), 0, REGIONS - 1).astype(jnp.int32),
        "heat_ratio": jnp.clip(jnp.exp(jax.random.uniform(arg_keys[5], (REGIONS,), jnp.float32, math.log(1.3), math.log(3.0))), 1.3, 3.0),
        "tracer": gaussian(arg_keys[6], (NZX, NZY, NZZ), 1.0, 6.0, ((0, 4), (1, 16), (2, 4)), jnp.float32),
    }


courant = 0.5
relax_weight = 0.9
shape_weights = (1.0 / 6.0, 2.0 / 3.0, 1.0 / 6.0)
slope_weights = (-1.0, 0.0, 1.0)

def spread_periodic(values, position, weights):
    earlier = jnp.roll(values, 1, position)
    first = weights[0] * values + weights[2] * earlier
    second = weights[1] * values
    stacked = jnp.stack([first, second], axis=position + 1)
    target = list(values.shape)
    target[position] = 2 * target[position]
    return stacked.reshape(target)

def node_term(values, slope_dim):
    result = values
    for position in range(3):
        weights = slope_weights if position == slope_dim else shape_weights
        result = spread_periodic(result, position, weights)
    return result

def relax_sweep(field):
    total = jnp.zeros_like(field)
    for position in (1, 2, 3):
        total = total + jnp.roll(field, 1, position) + jnp.roll(field, -1, position)
    return field + relax_weight * (total / 6.0 - field)

def reference(displacement, velocity, density, energy, region, heat_ratio, tracer):
    labels = jnp.arange(REGIONS, dtype=jnp.int32).reshape(-1, 1, 1, 1)
    member = (region[None] == labels).astype(jnp.float32)
    zone_ratio = lax.optimization_barrier(jnp.sum(member * heat_ratio.reshape(-1, 1, 1, 1), axis=0))
    pressure = (zone_ratio - 1.0) * density * energy
    sound = jnp.sqrt(zone_ratio * (zone_ratio - 1.0) * energy)
    time_step = courant / jnp.max(sound)
    forces = jnp.stack([node_term(pressure, slope_dim) for slope_dim in range(3)])
    masses = node_term(density, -1)
    new_velocity = velocity + time_step * forces / masses[None]
    moved = displacement + time_step * new_velocity
    relaxed_mesh = relax_sweep(relax_sweep(moved))
    motion = (relaxed_mesh - moved)[:, 1::2, 1::2, 1::2]
    donor_total = jnp.zeros_like(tracer)
    central_total = jnp.zeros_like(tracer)
    floor = tracer
    ceiling = tracer
    for position in range(3):
        behind = jnp.roll(tracer, 1, position)
        in_front = jnp.roll(tracer, -1, position)
        face_speed = 0.5 * (jnp.roll(motion[position], 1, position) + motion[position])
        donor = -(jnp.minimum(face_speed, 0.0) * behind + jnp.maximum(face_speed, 0.0) * tracer)
        central = -face_speed * 0.5 * (behind + tracer)
        donor_total = donor_total + (jnp.roll(donor, -1, position) - donor)
        central_total = central_total + (jnp.roll(central, -1, position) - central)
        floor = jnp.minimum(jnp.minimum(floor, behind), in_front)
        ceiling = jnp.maximum(jnp.maximum(ceiling, behind), in_front)
    low_order = tracer - donor_total
    high_order = tracer - central_total
    floor = jnp.minimum(floor, low_order)
    ceiling = jnp.maximum(ceiling, low_order)
    remapped = jnp.minimum(jnp.maximum(high_order, floor), ceiling)
    return (new_velocity, relaxed_mesh, remapped)
```

```python
import jax
import jax.numpy as jnp
from jax import lax
from jax.experimental import pallas as pl
from jax.experimental.pallas import tpu as pltpu
from jax.sharding import PartitionSpec as P

AXES = ("gx", "gy", "gz")
VM = pl.BlockSpec(memory_space=pltpu.VMEM)
SM = pl.BlockSpec(memory_space=pltpu.SMEM)
ANY = pl.BlockSpec(memory_space=pl.ANY)
F32 = jnp.float32

NX, NY, NZ = 8, 32, 256
MX, MY, MZ = 4, 16, 128

X_LOW = [(c, x) for c in range(3) for x in range(-3 if c == 0 else -2, 0)]
X_HIGH = [(c, x) for c in range(3) for x in range(NX, NX + (4 if c == 0 else 2))]
NL, NH = len(X_LOW), len(X_HIGH)
PLANES = [(c, x) for c in range(3) for x in range(-3 if c == 0 else -2, NX + (4 if c == 0 else 2))]
PLANE_AT = {key: i for i, key in enumerate(PLANES)}
NP = len(PLANES)


def low_rows(c, x):
    inside = 0 <= x < NX
    if c == 0:
        return 2 if inside else (1 if x in (-1, NX, NX + 1) else 0)
    if c == 1:
        return 3 if inside else {-1: 1, NX: 2, NX + 1: 1}.get(x, 0)
    return 2 if inside else (1 if x in (-1, NX) else 0)


def high_rows(c, x):
    inside = 0 <= x < NX
    if c == 0:
        return 2 if inside or x in (-1, NX, NX + 1) else (1 if x in (-2, NX + 2) else 0)
    if c == 1:
        return 4 if inside else {-1: 2, NX: 3, NX + 1: 2}.get(x, 0)
    return 2 if inside else (1 if x in (-1, NX) else 0)


def row_table(count):
    table, at = [], 0
    for c, x in PLANES:
        n = count(c, x)
        if n:
            table.append((c, x, at, n))
            at += n
    return table, at


Y_LOW, Y_LOW_N = row_table(low_rows)
Y_HIGH, Y_HIGH_N = row_table(high_rows)
EX = 2 * (MX + 4)
Y_LOW_SIZE = -(-(Y_LOW_N + EX + MX) // 8) * 8
Y_HIGH_SIZE = -(-(Y_HIGH_N + EX + MX) // 8) * 8
ZONE_SLOT = NP
TRACER_SLOT = NP + 2 * (MX + 4)


def step_of(r):
    top = jnp.max(jnp.max(r[...], axis=0, keepdims=True), axis=1, keepdims=True)
    return 0.5 / jnp.sqrt(top)


def first_kernel(ratio, d, v, rho, energy, region, tracer, low, high, most, pressure, zl, zh, sems):
    copies = []

    def copy(src, dst):
        cp = pltpu.make_async_copy(src, dst, sems.at[len(copies)])
        cp.start()
        copies.append(cp)

    at = 0
    for f, array in enumerate((d, v)):
        for c in range(3):
            n = 3 if c == 0 else 2
            off = f * NL + X_LOW.index((c, -n))
            copy(array.at[c, pl.ds(NX - n, n)], low.at[pl.ds(off, n)])
            n = 4 if c == 0 else 2
            off = f * NH + X_HIGH.index((c, NX))
            copy(array.at[c, pl.ds(0, n)], high.at[pl.ds(off, n)])
    top = jnp.zeros((MY, MZ), F32)
    for i in range(MX):
        reg = region[i]
        zone_ratio = jnp.where(
            reg < 2,
            jnp.where(reg == 0, ratio[0], ratio[1]),
            jnp.where(reg == 2, ratio[2], ratio[3]),
        )
        pr = (zone_ratio - 1.0) * rho[i] * energy[i]
        pressure[i] = pr
        top = jnp.maximum(top, zone_ratio * (zone_ratio - 1.0) * energy[i])
        if i < 2:
            zh[0, :MY, i * MZ : (i + 1) * MZ] = pr
            zh[0, MY:, i * MZ : (i + 1) * MZ] = rho[i]
        else:
            zl[0, :MY, (i - 2) * MZ : (i - 1) * MZ] = pr
            zl[0, MY:, (i - 2) * MZ : (i - 1) * MZ] = rho[i]
    zh[1, :MY, :MZ] = tracer[0]
    zl[1, :MY, :MZ] = tracer[MX - 1]
    copy(zl, low.at[pl.ds(2 * NL, 2)])
    copy(zh, high.at[pl.ds(2 * NH, 2)])
    top = jnp.max(jnp.max(top, axis=0, keepdims=True), axis=1, keepdims=True)
    most[...] = jnp.broadcast_to(top, most.shape)
    for cp in copies:
        cp.wait()


def zone_plane(i, own, low, high, which):
    if 0 <= i < MX:
        return own[which][i]
    rows = pl.ds(which * MY, MY)
    if i < 0:
        return low[2 * NL, rows, (i + 2) * MZ : (i + 3) * MZ]
    return high[2 * NH, rows, (i - MX) * MZ : (i - MX + 1) * MZ]


def node_pair(c, x, d, v, low, high):
    if 0 <= x < NX:
        return d.at[c, x], v.at[c, x]
    if x < 0:
        i = X_LOW.index((c, x))
        return low.at[i], low.at[NL + i]
    i = X_HIGH.index((c, x))
    return high.at[i], high.at[NH + i]


def second_kernel(r, d, v, low, high, pressure, rho, tracer, ylow, yhigh):
    step = step_of(r)
    for table, out, start, stop in ((Y_LOW, ylow, None, NY), (Y_HIGH, yhigh, 0, None)):
        for c, x, at, n in table:
            first = NY - n if start is None else 0
            a, b = node_pair(c, x, d, v, low, high)
            out[pl.ds(at, n), :] = a[pl.ds(first, n), :] + step * b[pl.ds(first, n), :]
    for out, base, first, edge in ((ylow, Y_LOW_N, MY - 2, MY - 1), (yhigh, Y_HIGH_N, 0, 0)):
        for i in range(-2, MX + 2):
            for which in range(2):
                lanes = slice(which * MZ, (which + 1) * MZ)
                out[pl.ds(base + 2 * (i + 2), 2), lanes] = zone_plane(
                    i, (pressure, rho), low, high, which
                )[first : first + 2]
        for i in range(MX):
            out[pl.ds(base + EX + i, 1), :MZ] = tracer[i, pl.ds(edge, 1), :]


def third_kernel(
    r, d, v, low, high, pressure, rho, tracer, ylow, yhigh, ext, zones, zlow, zhigh
):
    step = step_of(r)
    lows = {(c, x): (at, n) for c, x, at, n in Y_LOW}
    highs = {(c, x): (at, n) for c, x, at, n in Y_HIGH}
    for e, (c, x) in enumerate(PLANES):
        a, b = node_pair(c, x, d, v, low, high)
        ext[e, pl.ds(8, NY), :] = a[...] + step * b[...]
        if (c, x) in lows:
            at, n = lows[c, x]
            ext[e, pl.ds(8 - n, n), :] = ylow[pl.ds(at, n), :]
        if (c, x) in highs:
            at, n = highs[c, x]
            ext[e, pl.ds(8 + NY, n), :] = yhigh[pl.ds(at, n), :]
    for which in range(2):
        lanes = slice(which * MZ, (which + 1) * MZ)
        for i in range(-2, MX + 2):
            k = which * (MX + 4) + i + 2
            zones[k, pl.ds(4, MY), :] = zone_plane(i, (pressure, rho), low, high, which)
            zones[k, pl.ds(2, 2), :] = ylow[pl.ds(Y_LOW_N + 2 * (i + 2), 2), lanes]
            zones[k, pl.ds(4 + MY, 2), :] = yhigh[pl.ds(Y_HIGH_N + 2 * (i + 2), 2), lanes]
    lane = lax.broadcasted_iota(jnp.int32, (1, 128), 1)
    for tile in range(2):
        zlow[tile] = jnp.zeros((48, 128), F32)
        zhigh[tile] = jnp.zeros((48, 128), F32)
        for s in range(32):
            slot = tile * 32 + s
            if slot >= TRACER_SLOT + MX:
                break
            if slot < ZONE_SLOT:
                left, right, n = ext[slot, :, :128], ext[slot, :, 128:], 48
            elif slot < TRACER_SLOT:
                left = right = zones[slot - ZONE_SLOT]
                n = 24
            else:
                left = right = tracer[slot - TRACER_SLOT]
                n = MY
            here = (lane >= 4 * s) & (lane < 4 * s + 4)
            rows = pl.ds(0, n)
            zhigh[tile, rows] = jnp.where(here, roll(left, 4 * s, 1), zhigh[tile, rows])
            zlow[tile, rows] = jnp.where(here, roll(right, 4 * s + 4, 1), zlow[tile, rows])


def roll(value, by, axis):
    by %= value.shape[axis]
    return pltpu.roll(value, by, axis) if by else value


def pieces(value):
    first = value.astype(jnp.bfloat16)
    rest = value - first.astype(F32)
    second = rest.astype(jnp.bfloat16)
    return first, second, (rest - second.astype(F32)).astype(jnp.bfloat16)


def product(parts, matrix):
    total = None
    for part in parts:
        term = jnp.dot(part, matrix, preferred_element_type=F32)
        total = term if total is None else total + term
    return total


def last_kernel(
    r, v, ext, zones, tracer, low, high, ylow, yhigh, zlow, zhigh,
    velocity, relaxed, remapped,
    moved, once, pz, qx, qy, qz, qm, moves, gathered, result, tz,
):
    step = step_of(r)
    lane = lax.broadcasted_iota(jnp.int32, (1, 128), 1)

    def beside(slot, n, fill):
        tile, s = divmod(slot, 32)
        rows = pl.ds(0, n)
        after = roll(zhigh[tile, rows], -4 * s, 1)
        before = roll(zlow[tile, rows], 124 - 4 * s, 1)
        return jnp.where(lane < 4, after, jnp.where(lane >= 124, before, fill))

    for k in range(2 * (MX + 4)):
        pz[k, :, :MZ] = zones[k]
        pz[k, :, MZ:] = beside(ZONE_SLOT + k, 24, 0.0 if k < MX + 4 else 1.0)
    k = lax.broadcasted_iota(jnp.int32, (2 * MZ, 384), 0)
    n = lax.broadcasted_iota(jnp.int32, (2 * MZ, 384), 1)
    a = jnp.where(n < 320, n, n - 384) - 2 * jnp.where(k < 192, k, k - 256)
    shape = jnp.where((a == 0) | (a == 2), 1.0, jnp.where(a == 1, 4.0, 0.0)).astype(jnp.bfloat16)
    slope = jnp.where(a == 0, -1.0, jnp.where(a == 2, 1.0, 0.0)).astype(jnp.bfloat16)
    half = (MX + 4) * 24
    both = pz[...].reshape(2 * half, 2 * MZ)
    spread = product(pieces(both), shape)
    slanted = product(pieces(both[:half]), slope)
    even, odd = pl.ds(0, 24, stride=2), pl.ds(1, 24, stride=2)

    def interleave(q, i, first, second):
        for t in range(3):
            lanes = slice(128 * t, 128 * t + 128)
            q[3 * i + t, even, :] = first[:, lanes]
            q[3 * i + t, odd, :] = second[:, lanes]

    def whole(q, i):
        return jnp.concatenate([q[3 * i + t] for t in range(3)], axis=1)

    for i in range(MX + 4):
        now = spread[24 * i : 24 * i + 24]
        before = roll(now, 1, 0)
        interleave(qx, i, now + before, 4.0 * now)
        interleave(qy, i, before - now, jnp.zeros((24, 384), F32))
        now = slanted[24 * i : 24 * i + 24]
        interleave(qz, i, now + roll(now, 1, 0), 4.0 * now)
        now = spread[half + 24 * i : half + 24 * i + 24]
        interleave(qm, i, now + roll(now, 1, 0), 4.0 * now)
    for x in range(-3, NX + 4):
        i = x // 2 + 2
        mass = whole(qm, i)
        mass = mass + whole(qm, i - 1) if x % 2 == 0 else 4.0 * mass
        push = 6.0 * step / mass
        for c in range(3):
            if (c, x) not in PLANE_AT:
                continue
            e = PLANE_AT[c, x]
            if c == 0:
                force = whole(qx, i - 1) - whole(qx, i) if x % 2 == 0 else None
            else:
                q = qy if c == 1 else qz
                force = whole(q, i)
                force = force + whole(q, i - 1) if x % 2 == 0 else 4.0 * force
            third = beside(e, 48, 0.0)
            if force is None:
                moved[e, :, :NZ] = ext[e]
                moved[e, :, NZ:] = third
                if 0 <= x < NX:
                    velocity[c, x] = v[c, x]
            else:
                gain = force * push
                moved[e, :, :NZ] = ext[e] + step * gain[:, :NZ]
                moved[e, :, NZ:] = third + step * gain[:, NZ:]
                if 0 <= x < NX:
                    velocity[c, x] = v[c, x] + gain[8 : 8 + NY, :NZ]

    def sweep(ref, e):
        now = ref[e]
        total = ref[e - 1] + ref[e + 1]
        total = total + (roll(now, 1, 0) + roll(now, -1, 0))
        total = total + (roll(now, 1, 1) + roll(now, -1, 1))
        return 0.1 * now + 0.15 * total

    for e, (c, x) in enumerate(PLANES):
        if (c, x - 1) in PLANE_AT and (c, x + 1) in PLANE_AT:
            once[e] = sweep(moved, e)
    at = 0
    for e, (c, x) in enumerate(PLANES):
        inside = 0 <= x < NX
        if not inside and not (c == 0 and x in (-1, NX + 1)):
            continue
        twice = sweep(once, e)
        if inside:
            relaxed[c, x] = twice[8 : 8 + NY, :NZ]
        if x % 2:
            motion = twice - moved[e]
            first, count = (7, 18) if c == 1 else (9, 16)
            for t in range(3):
                lanes = slice(128 * t, 128 * t + 128)
                moves[t] = motion[:, lanes]
                gathered[pl.ds(at, count), lanes] = moves[t, pl.ds(first, count, stride=2), :]
            if c == 1:
                gathered[pl.ds(at + 18, 6), :] = jnp.zeros((6, 384), F32)
            at += 24 if c == 1 else 16
    n = lax.broadcasted_iota(jnp.int32, (384, 2 * MZ), 0)
    k = lax.broadcasted_iota(jnp.int32, (384, 2 * MZ), 1)
    node = jnp.where(n < 320, n, n - 384)
    chosen = (node == 2 * jnp.where(k < 192, k, k - 256) + 1).astype(F32).astype(jnp.bfloat16)
    result[...] = product(pieces(gathered[...]), chosen)

    def flux(speed, behind, here):
        donor = -(jnp.minimum(speed, 0.0) * behind + jnp.maximum(speed, 0.0) * here)
        return donor, -speed * 0.5 * (behind + here)

    y0, z0 = (MX + 2) * 16, (MX + 2) * 16 + MX * 24
    for i in range(MX):
        now = tracer[i]
        tz[pl.ds(8, MY), :] = now
        tz[pl.ds(7, 1), :] = ylow[pl.ds(Y_LOW_N + EX + i, 1), :MZ]
        tz[pl.ds(8 + MY, 1), :] = yhigh[pl.ds(Y_HIGH_N + EX + i, 1), :MZ]
        side = beside(TRACER_SLOT + i, MY, 0.0)
        edge = result[pl.ds(z0 + 16 * i, 16), MZ:]
        middle = result[pl.ds(z0 + 16 * i, 16), :MZ]
        around = (
            (
                tracer[i - 1] if i else low[2 * NL + 1, :MY, :MZ],
                tracer[i + 1] if i < MX - 1 else high[2 * NH + 1, :MY, :MZ],
                result[pl.ds(16 * i, 16), :MZ],
                result[pl.ds(16 * (i + 1), 16), :MZ],
                result[pl.ds(16 * (i + 2), 16), :MZ],
            ),
            (
                tz[pl.ds(7, MY), :],
                tz[pl.ds(9, MY), :],
                result[pl.ds(y0 + 24 * i, 16), :MZ],
                result[pl.ds(y0 + 24 * i + 1, 16), :MZ],
                result[pl.ds(y0 + 24 * i + 2, 16), :MZ],
            ),
            (
                jnp.where(lane == 0, roll(side, 1, 1), roll(now, 1, 1)),
                jnp.where(lane == MZ - 1, roll(side, -1, 1), roll(now, -1, 1)),
                jnp.where(lane == 0, roll(edge, 1, 1), roll(middle, 1, 1)),
                middle,
                jnp.where(lane == MZ - 1, roll(edge, -1, 1), roll(middle, -1, 1)),
            ),
        )
        donors = centrals = None
        floor = ceiling = now
        for behind, front, m0, m1, m2 in around:
            d0, c0 = flux(0.5 * (m0 + m1), behind, now)
            d1, c1 = flux(0.5 * (m1 + m2), now, front)
            donors = d1 - d0 if donors is None else donors + (d1 - d0)
            centrals = c1 - c0 if centrals is None else centrals + (c1 - c0)
            floor = jnp.minimum(jnp.minimum(floor, behind), front)
            ceiling = jnp.maximum(jnp.maximum(ceiling, behind), front)
        low_order = now - donors
        high_order = now - centrals
        floor = jnp.minimum(floor, low_order)
        ceiling = jnp.maximum(ceiling, low_order)
        remapped[i] = jnp.minimum(jnp.maximum(high_order, floor), ceiling)


def shape_of(*dims):
    return jax.ShapeDtypeStruct(dims, F32)


def moved_along(block, axis, by):
    n = lax.axis_size(axis)
    return lax.ppermute(block, axis, [(i, (i + by) % n) for i in range(n)])


def on_device(displacement, velocity, density, energy, region, heat_ratio, tracer):
    n_devices = lax.axis_size(AXES)
    low, high, most, pressure = pl.pallas_call(
        first_kernel,
        name="first",
        in_specs=[SM, ANY, ANY, VM, VM, VM, VM],
        out_specs=[ANY, ANY, VM, VM],
        out_shape=[
            shape_of(2 * NL + 2, NY, NZ),
            shape_of(2 * NH + 2, NY, NZ),
            shape_of(n_devices, 128),
            shape_of(MX, MY, MZ),
        ],
        scratch_shapes=[
            pltpu.VMEM((2, NY, NZ), F32),
            pltpu.VMEM((2, NY, NZ), F32),
            pltpu.SemaphoreType.DMA((14,)),
        ],
    )(heat_ratio, displacement, velocity, density, energy, region, tracer)
    low = moved_along(low, "gx", 1)
    high = moved_along(high, "gx", -1)
    r = lax.all_to_all(most, AXES, 0, 0, tiled=True)
    ylow, yhigh = pl.pallas_call(
        second_kernel,
        name="second",
        in_specs=[VM] * 8,
        out_specs=[VM] * 2,
        out_shape=[shape_of(Y_LOW_SIZE, NZ), shape_of(Y_HIGH_SIZE, NZ)],
    )(r, displacement, velocity, low, high, pressure, density, tracer)
    ylow = moved_along(ylow, "gy", 1)
    yhigh = moved_along(yhigh, "gy", -1)
    ext, zones, zlow, zhigh = pl.pallas_call(
        third_kernel,
        name="third",
        in_specs=[VM] * 10,
        out_specs=[VM] * 4,
        out_shape=[
            shape_of(NP, 48, NZ),
            shape_of(2 * (MX + 4), 24, MZ),
            shape_of(2, 48, 128),
            shape_of(2, 48, 128),
        ],
    )(r, displacement, velocity, low, high, pressure, density, tracer, ylow, yhigh)
    zlow = moved_along(zlow, "gz", 1)
    zhigh = moved_along(zhigh, "gz", -1)
    q = pltpu.VMEM((3 * (MX + 4), 48, 128), F32)
    return pl.pallas_call(
        last_kernel,
        name="last",
        in_specs=[VM] * 11,
        out_specs=[VM] * 3,
        out_shape=[shape_of(3, NX, NY, NZ), shape_of(3, NX, NY, NZ), shape_of(MX, MY, MZ)],
        scratch_shapes=[
            pltpu.VMEM((NP, 48, 384), F32),
            pltpu.VMEM((NP, 48, 384), F32),
            pltpu.VMEM((2 * (MX + 4), 24, 2 * MZ), F32),
            q, q, q, q,
            pltpu.VMEM((3, 48, 128), F32),
            pltpu.VMEM((256, 384), F32),
            pltpu.VMEM((256, 2 * MZ), F32),
            pltpu.VMEM((MY + 16, MZ), F32),
        ],
    )(r, velocity, ext, zones, tracer, low, high, ylow, yhigh, zlow, zhigh)


def solution(mesh):
    node, zone = P(None, "gx", "gy", "gz"), P("gx", "gy", "gz")
    return jax.shard_map(
        on_device,
        mesh=mesh,
        in_specs=(node, node, zone, zone, zone, P(), zone),
        out_specs=(node, node, zone),
        check_vma=False,
    )
```

```python
import jax
import jax.numpy as jnp
from jax import lax
from jax.experimental import pallas as pl
from jax.experimental.pallas import tpu as pltpu
from jax.sharding import PartitionSpec as P


AXES = ("gx", "gy", "gz")
VM = pl.BlockSpec(memory_space=pltpu.VMEM)
SM = pl.BlockSpec(memory_space=pltpu.SMEM)
F32 = jnp.float32

NX, NY, NZ = 8, 32, 256
MX, MY, MZ = 4, 16, 128

X_LOW = [(c, x) for c in range(3) for x in range(-3 if c == 0 else -2, 0)]
X_HIGH = [(c, x) for c in range(3) for x in range(NX, NX + (4 if c == 0 else 2))]
NL, NH = len(X_LOW), len(X_HIGH)
PLANES = [(c, x) for c in range(3) for x in range(-3 if c == 0 else -2, NX + (4 if c == 0 else 2))]
PLANE_AT = {key: i for i, key in enumerate(PLANES)}
NP = len(PLANES)


def low_rows(c, x):
    inside = 0 <= x < NX
    if c == 0:
        return 2 if inside else (1 if x in (-1, NX, NX + 1) else 0)
    if c == 1:
        return 3 if inside else {-1: 1, NX: 2, NX + 1: 1}.get(x, 0)
    return 2 if inside else (1 if x in (-1, NX) else 0)


def high_rows(c, x):
    inside = 0 <= x < NX
    if c == 0:
        return 2 if inside or x in (-1, NX, NX + 1) else (1 if x in (-2, NX + 2) else 0)
    if c == 1:
        return 4 if inside else {-1: 2, NX: 3, NX + 1: 2}.get(x, 0)
    return 2 if inside else (1 if x in (-1, NX) else 0)


def row_table(count):
    table, at = [], 0
    for c, x in PLANES:
        n = count(c, x)
        if n:
            table.append((c, x, at, n))
            at += n
    return table, at


Y_LOW, Y_LOW_N = row_table(low_rows)
Y_HIGH, Y_HIGH_N = row_table(high_rows)
LOW_ZONES, HIGH_ZONES = 2 * Y_LOW_N, 2 * Y_HIGH_N
EX = 2 * (MX + 4)
Y_LOW_SIZE = -(-(LOW_ZONES + EX + MX) // 8) * 8
Y_HIGH_SIZE = -(-(HIGH_ZONES + EX + MX) // 8) * 8
Z_PLANES = [(c, x) for c, x in PLANES if -2 <= x <= NX + (2 if c == 0 else 1)]
ZN = len(Z_PLANES)
ZONE_SLOT = 2 * ZN
TRACER_SLOT = ZONE_SLOT + 2 * (MX + 4)
Z_TILES = -(-(TRACER_SLOT + MX) // 32)


def step_of(r):
    top = jnp.max(jnp.max(r[...], axis=0, keepdims=True), axis=1, keepdims=True)
    return 0.5 / jnp.sqrt(top)


def first_kernel(ratio, d, v, rho, energy, region, tracer, low, high, most, pressure):
    for f, array in enumerate((d, v)):
        for table, size, out, shift in ((X_LOW, NL, low, NX), (X_HIGH, NH, high, -NX)):
            for at, (c, x) in enumerate(table):
                out[f * size + at] = array[c, x + shift]
    top = jnp.zeros((MY, MZ), F32)
    for i in range(MX):
        reg = region[i]
        zone_ratio = jnp.where(
            reg < 2,
            jnp.where(reg == 0, ratio[0], ratio[1]),
            jnp.where(reg == 2, ratio[2], ratio[3]),
        )
        pr = (zone_ratio - 1.0) * rho[i] * energy[i]
        pressure[i] = pr
        top = jnp.maximum(top, zone_ratio * (zone_ratio - 1.0) * energy[i])
        out, at = (high, 2 * NH) if i < 2 else (low, 2 * NL)
        lanes = slice(i % 2 * MZ, (i % 2 + 1) * MZ)
        out[at, :MY, lanes] = pr
        out[at, MY:, lanes] = rho[i]
    high[2 * NH + 1, :MY, :MZ] = tracer[0]
    low[2 * NL + 1, :MY, :MZ] = tracer[MX - 1]
    top = jnp.max(jnp.max(top, axis=0, keepdims=True), axis=1, keepdims=True)
    most[...] = jnp.broadcast_to(top, most.shape)


def zone_plane(i, own, low, high, which):
    if 0 <= i < MX:
        return own[which][i]
    rows = pl.ds(which * MY, MY)
    if i < 0:
        return low[2 * NL, rows, (i + 2) * MZ : (i + 3) * MZ]
    return high[2 * NH, rows, (i - MX) * MZ : (i - MX + 1) * MZ]


def node_pair(c, x, d, v, low, high):
    if 0 <= x < NX:
        return d.at[c, x], v.at[c, x]
    if x < 0:
        i = X_LOW.index((c, x))
        return low.at[i], low.at[NL + i]
    i = X_HIGH.index((c, x))
    return high.at[i], high.at[NH + i]


def second_kernel(d, v, low, high, pressure, rho, tracer, ylow, yhigh):
    for table, size, out, top in ((Y_LOW, Y_LOW_N, ylow, True), (Y_HIGH, Y_HIGH_N, yhigh, False)):
        for c, x, at, n in table:
            first = NY - n if top else 0
            for f, plane in enumerate(node_pair(c, x, d, v, low, high)):
                out[pl.ds(f * size + at, n), :] = plane[pl.ds(first, n), :]
    for out, base, first, edge in ((ylow, LOW_ZONES, MY - 2, MY - 1), (yhigh, HIGH_ZONES, 0, 0)):
        for i in range(-2, MX + 2):
            for which in range(2):
                lanes = slice(which * MZ, (which + 1) * MZ)
                out[pl.ds(base + 2 * (i + 2), 2), lanes] = zone_plane(
                    i, (pressure, rho), low, high, which
                )[first : first + 2]
        for i in range(MX):
            out[pl.ds(base + EX + i, 1), :MZ] = tracer[i, pl.ds(edge, 1), :]


LOW_AT = {(c, x): (at, n) for c, x, at, n in Y_LOW}
HIGH_AT = {(c, x): (at, n) for c, x, at, n in Y_HIGH}


def zone_block(zones, pressure, rho, low, high, ylow, yhigh):
    for which in range(2):
        lanes = slice(which * MZ, (which + 1) * MZ)
        for i in range(-2, MX + 2):
            k = which * (MX + 4) + i + 2
            zones[k, pl.ds(4, MY), :MZ] = zone_plane(i, (pressure, rho), low, high, which)
            zones[k, pl.ds(2, 2), :MZ] = ylow[pl.ds(LOW_ZONES + 2 * (i + 2), 2), lanes]
            zones[k, pl.ds(4 + MY, 2), :MZ] = yhigh[pl.ds(HIGH_ZONES + 2 * (i + 2), 2), lanes]


def third_kernel(
    d, v, low, high, pressure, rho, tracer, ylow, yhigh, zlow, zhigh, zones, lefts, rights
):
    zone_block(zones, pressure, rho, low, high, ylow, yhigh)
    lane = lax.broadcasted_iota(jnp.int32, (1, 128), 1)
    for tile in range(Z_TILES):
        zlow[tile] = jnp.zeros((48, 128), F32)
        zhigh[tile] = jnp.zeros((48, 128), F32)
    for slot in range(TRACER_SLOT + MX):
        tile, s = divmod(slot, 32)
        here = (lane >= 4 * s) & (lane < 4 * s + 4)

        def put(rows, left, right):
            zhigh[tile, rows] = jnp.where(here, roll(left, 4 * s, 1), zhigh[tile, rows])
            zlow[tile, rows] = jnp.where(here, roll(right, 4 * s + 4, 1), zlow[tile, rows])

        if slot < ZONE_SLOT:
            f, e = divmod(slot, ZN)
            c, x = Z_PLANES[e]
            plane = node_pair(c, x, d, v, low, high)[f]
            put(pl.ds(8, NY), plane[:, :128], plane[:, 128:])
            if (c, x) in LOW_AT:
                at, n = LOW_AT[c, x]
                lefts[pl.ds(8 - n, n), :] = ylow[pl.ds(f * Y_LOW_N + at, n), :]
                put(pl.ds(0, 8), lefts[:, :128], lefts[:, 128:])
            if (c, x) in HIGH_AT:
                at, n = HIGH_AT[c, x]
                rights[pl.ds(0, n), :] = yhigh[pl.ds(f * Y_HIGH_N + at, n), :]
                put(pl.ds(8 + NY, 8), rights[:, :128], rights[:, 128:])
        elif slot < TRACER_SLOT:
            put(pl.ds(0, 24), zones[slot - ZONE_SLOT], zones[slot - ZONE_SLOT])
        else:
            put(pl.ds(0, MY), tracer[slot - TRACER_SLOT], tracer[slot - TRACER_SLOT])


def roll(value, by, axis):
    by %= value.shape[axis]
    return pltpu.roll(value, by, axis) if by else value


def pieces(value):
    first = value.astype(jnp.bfloat16)
    rest = value - first.astype(F32)
    second = rest.astype(jnp.bfloat16)
    return first, second, (rest - second.astype(F32)).astype(jnp.bfloat16)


def product(parts, matrix):
    total = None
    for part in parts:
        term = jnp.dot(part, matrix, preferred_element_type=F32)
        total = term if total is None else total + term
    return total


def last_kernel(
    r, d, v, low, high, pressure, rho, tracer, ylow, yhigh, zlow, zhigh,
    velocity, relaxed, remapped,
    moved, once, pz, qx, qy, qz, qm, moves, gathered, result, tz,
):
    step = step_of(r)
    lane = lax.broadcasted_iota(jnp.int32, (1, 128), 1)

    def beside(slot, n, fill):
        tile, s = divmod(slot, 32)
        rows = pl.ds(0, n)
        after = roll(zhigh[tile, rows], -4 * s, 1)
        before = roll(zlow[tile, rows], 124 - 4 * s, 1)
        return jnp.where(lane < 4, after, jnp.where(lane >= 124, before, fill))

    zone_block(pz, pressure, rho, low, high, ylow, yhigh)
    for k in range(2 * (MX + 4)):
        pz[k, :, MZ:] = beside(ZONE_SLOT + k, 24, 0.0 if k < MX + 4 else 1.0)
    k = lax.broadcasted_iota(jnp.int32, (2 * MZ, 384), 0)
    n = lax.broadcasted_iota(jnp.int32, (2 * MZ, 384), 1)
    a = jnp.where(n < 320, n, n - 384) - 2 * jnp.where(k < 192, k, k - 256)
    shape = jnp.where((a == 0) | (a == 2), 1.0, jnp.where(a == 1, 4.0, 0.0)).astype(jnp.bfloat16)
    slope = jnp.where(a == 0, -1.0, jnp.where(a == 2, 1.0, 0.0)).astype(jnp.bfloat16)
    half = (MX + 4) * 24
    both = pz[...].reshape(2 * half, 2 * MZ)
    spread = product(pieces(both), shape)
    slanted = product(pieces(both[:half]), slope)
    even, odd = pl.ds(0, 24, stride=2), pl.ds(1, 24, stride=2)

    def interleave(q, i, first, second):
        for t in range(3):
            lanes = slice(128 * t, 128 * t + 128)
            q[3 * i + t, even, :] = first[:, lanes]
            q[3 * i + t, odd, :] = second[:, lanes]

    def whole(q, i):
        return jnp.concatenate([q[3 * i + t] for t in range(3)], axis=1)

    for i in range(MX + 4):
        now = spread[24 * i : 24 * i + 24]
        before = roll(now, 1, 0)
        interleave(qx, i, now + before, 4.0 * now)
        interleave(qy, i, before - now, jnp.zeros((24, 384), F32))
        now = slanted[24 * i : 24 * i + 24]
        interleave(qz, i, now + roll(now, 1, 0), 4.0 * now)
        now = spread[half + 24 * i : half + 24 * i + 24]
        interleave(qm, i, now + roll(now, 1, 0), 4.0 * now)
    for x in range(-3, NX + 4):
        i = x // 2 + 2
        mass = whole(qm, i)
        mass = mass + whole(qm, i - 1) if x % 2 == 0 else 4.0 * mass
        push = 6.0 * step / mass
        for c in range(3):
            if (c, x) not in PLANE_AT:
                continue
            e = PLANE_AT[c, x]
            if c == 0:
                force = whole(qx, i - 1) - whole(qx, i) if x % 2 == 0 else None
            else:
                q = qy if c == 1 else qz
                force = whole(q, i)
                force = force + whole(q, i - 1) if x % 2 == 0 else 4.0 * force
            here, there = node_pair(c, x, d, v, low, high)
            moved[e, pl.ds(8, NY), :NZ] = here[...] + step * there[...]
            if (c, x) in LOW_AT:
                at, n = LOW_AT[c, x]
                moved[e, pl.ds(8 - n, n), :NZ] = (
                    ylow[pl.ds(at, n), :] + step * ylow[pl.ds(Y_LOW_N + at, n), :]
                )
            if (c, x) in HIGH_AT:
                at, n = HIGH_AT[c, x]
                moved[e, pl.ds(8 + NY, n), :NZ] = (
                    yhigh[pl.ds(at, n), :] + step * yhigh[pl.ds(Y_HIGH_N + at, n), :]
                )
            if (c, x) in Z_PLANES:
                z = Z_PLANES.index((c, x))
                moved[e, :, NZ:] = beside(z, 48, 0.0) + step * beside(ZN + z, 48, 0.0)
            else:
                moved[e, :, NZ:] = jnp.zeros((48, 128), F32)
            if force is not None:
                gain = force * push
                moved[e] = moved[e] + step * gain
            if 0 <= x < NX:
                new = v[c, x]
                velocity[c, x] = new if force is None else new + gain[8 : 8 + NY, :NZ]

    def sweep(ref, e):
        now = ref[e]
        total = ref[e - 1] + ref[e + 1]
        total = total + (roll(now, 1, 0) + roll(now, -1, 0))
        total = total + (roll(now, 1, 1) + roll(now, -1, 1))
        return 0.1 * now + 0.15 * total

    for e, (c, x) in enumerate(PLANES):
        if (c, x - 1) in PLANE_AT and (c, x + 1) in PLANE_AT:
            once[e] = sweep(moved, e)
    at = 0
    for e, (c, x) in enumerate(PLANES):
        inside = 0 <= x < NX
        if not inside and not (c == 0 and x in (-1, NX + 1)):
            continue
        twice = sweep(once, e)
        if inside:
            relaxed[c, x] = twice[8 : 8 + NY, :NZ]
        if x % 2:
            motion = twice - moved[e]
            first, count = (7, 18) if c == 1 else (9, 16)
            for t in range(3):
                lanes = slice(128 * t, 128 * t + 128)
                moves[t] = motion[:, lanes]
                gathered[pl.ds(at, count), lanes] = moves[t, pl.ds(first, count, stride=2), :]
            if c == 1:
                gathered[pl.ds(at + 18, 6), :] = jnp.zeros((6, 384), F32)
            at += 24 if c == 1 else 16
    n = lax.broadcasted_iota(jnp.int32, (384, 2 * MZ), 0)
    k = lax.broadcasted_iota(jnp.int32, (384, 2 * MZ), 1)
    node = jnp.where(n < 320, n, n - 384)
    chosen = (node == 2 * jnp.where(k < 192, k, k - 256) + 1).astype(F32).astype(jnp.bfloat16)
    result[...] = product(pieces(gathered[...]), chosen)

    def flux(speed, behind, here):
        donor = -(jnp.minimum(speed, 0.0) * behind + jnp.maximum(speed, 0.0) * here)
        return donor, -speed * 0.5 * (behind + here)

    y0, z0 = (MX + 2) * 16, (MX + 2) * 16 + MX * 24
    for i in range(MX):
        now = tracer[i]
        tz[pl.ds(8, MY), :] = now
        tz[pl.ds(7, 1), :] = ylow[pl.ds(LOW_ZONES + EX + i, 1), :MZ]
        tz[pl.ds(8 + MY, 1), :] = yhigh[pl.ds(HIGH_ZONES + EX + i, 1), :MZ]
        side = beside(TRACER_SLOT + i, MY, 0.0)
        edge = result[pl.ds(z0 + 16 * i, 16), MZ:]
        middle = result[pl.ds(z0 + 16 * i, 16), :MZ]
        around = (
            (
                tracer[i - 1] if i else low[2 * NL + 1, :MY, :MZ],
                tracer[i + 1] if i < MX - 1 else high[2 * NH + 1, :MY, :MZ],
                result[pl.ds(16 * i, 16), :MZ],
                result[pl.ds(16 * (i + 1), 16), :MZ],
                result[pl.ds(16 * (i + 2), 16), :MZ],
            ),
            (
                tz[pl.ds(7, MY), :],
                tz[pl.ds(9, MY), :],
                result[pl.ds(y0 + 24 * i, 16), :MZ],
                result[pl.ds(y0 + 24 * i + 1, 16), :MZ],
                result[pl.ds(y0 + 24 * i + 2, 16), :MZ],
            ),
            (
                jnp.where(lane == 0, roll(side, 1, 1), roll(now, 1, 1)),
                jnp.where(lane == MZ - 1, roll(side, -1, 1), roll(now, -1, 1)),
                jnp.where(lane == 0, roll(edge, 1, 1), roll(middle, 1, 1)),
                middle,
                jnp.where(lane == MZ - 1, roll(edge, -1, 1), roll(middle, -1, 1)),
            ),
        )
        donors = centrals = None
        floor = ceiling = now
        for behind, front, m0, m1, m2 in around:
            d0, c0 = flux(0.5 * (m0 + m1), behind, now)
            d1, c1 = flux(0.5 * (m1 + m2), now, front)
            donors = d1 - d0 if donors is None else donors + (d1 - d0)
            centrals = c1 - c0 if centrals is None else centrals + (c1 - c0)
            floor = jnp.minimum(jnp.minimum(floor, behind), front)
            ceiling = jnp.maximum(jnp.maximum(ceiling, behind), front)
        low_order = now - donors
        high_order = now - centrals
        floor = jnp.minimum(floor, low_order)
        ceiling = jnp.maximum(ceiling, low_order)
        remapped[i] = jnp.minimum(jnp.maximum(high_order, floor), ceiling)


def shape_of(*dims):
    return jax.ShapeDtypeStruct(dims, F32)


def local_of(*dims):
    return pltpu.VMEM(dims, F32)


def on_chip(array):
    return pltpu.with_memory_space_constraint(array, pltpu.VMEM)


def moved_along(block, axis, by):
    n = lax.axis_size(axis)
    return on_chip(lax.ppermute(block, axis, [(i, (i + by) % n) for i in range(n)]))


def pack_y(*operands):
    return pl.pallas_call(
        second_kernel,
        name="second",
        compiler_params=pltpu.CompilerParams(vmem_limit_bytes=8 << 20),
        in_specs=[VM] * 7,
        out_specs=[VM] * 2,
        out_shape=[local_of(Y_LOW_SIZE, NZ), local_of(Y_HIGH_SIZE, NZ)],
    )(*operands)


def on_device(displacement, velocity, density, energy, region, heat_ratio, tracer):
    n_devices = lax.axis_size(AXES)
    displacement, velocity, density, energy, region, tracer = (
        on_chip(array) for array in (displacement, velocity, density, energy, region, tracer)
    )
    low, high, most, pressure = pl.pallas_call(
        first_kernel,
        name="first",
        compiler_params=pltpu.CompilerParams(vmem_limit_bytes=8 << 20),
        in_specs=[SM] + [VM] * 6,
        out_specs=[VM] * 4,
        out_shape=[
            local_of(2 * NL + 2, NY, NZ),
            local_of(2 * NH + 2, NY, NZ),
            local_of(n_devices, 128),
            local_of(MX, MY, MZ),
        ],
    )(heat_ratio, displacement, velocity, density, energy, region, tracer)
    low = moved_along(low, "gx", 1)
    high = moved_along(high, "gx", -1)
    r = on_chip(lax.all_to_all(most, AXES, 0, 0, tiled=True))
    ylow, yhigh = pack_y(displacement, velocity, low, high, pressure, density, tracer)
    ylow = moved_along(ylow, "gy", 1)
    yhigh = moved_along(yhigh, "gy", -1)
    zlow, zhigh = pl.pallas_call(
        third_kernel,
        name="third",
        compiler_params=pltpu.CompilerParams(vmem_limit_bytes=8 << 20),
        in_specs=[VM] * 9,
        out_specs=[VM] * 2,
        out_shape=[local_of(Z_TILES, 48, 128)] * 2,
        scratch_shapes=[
            pltpu.VMEM((2 * (MX + 4), 24, MZ), F32),
            pltpu.VMEM((8, NZ), F32),
            pltpu.VMEM((8, NZ), F32),
        ],
    )(displacement, velocity, low, high, pressure, density, tracer, ylow, yhigh)
    zlow = moved_along(zlow, "gz", 1)
    zhigh = moved_along(zhigh, "gz", -1)
    q = pltpu.VMEM((3 * (MX + 4), 48, 128), F32)
    return pl.pallas_call(
        last_kernel,
        name="last",
        compiler_params=pltpu.CompilerParams(vmem_limit_bytes=30 << 20),
        in_specs=[VM] * 12,
        out_specs=[VM] * 3,
        out_shape=[shape_of(3, NX, NY, NZ), shape_of(3, NX, NY, NZ), shape_of(MX, MY, MZ)],
        scratch_shapes=[
            pltpu.VMEM((NP, 48, 384), F32),
            pltpu.VMEM((NP, 48, 384), F32),
            pltpu.VMEM((2 * (MX + 4), 24, 2 * MZ), F32),
            q, q, q, q,
            pltpu.VMEM((3, 48, 128), F32),
            pltpu.VMEM((256, 384), F32),
            pltpu.VMEM((256, 2 * MZ), F32),
            pltpu.VMEM((MY + 16, MZ), F32),
        ],
    )(
        r, displacement, velocity, low, high, pressure, density, tracer, ylow, yhigh, zlow, zhigh
    )


def solution(mesh):
    node, zone = P(None, "gx", "gy", "gz"), P("gx", "gy", "gz")
    return jax.shard_map(
        on_device,
        mesh=mesh,
        in_specs=(node, node, zone, zone, zone, P(), zone),
        out_specs=(node, node, zone),
        check_vma=False,
    )
```

```python
import jax
import jax.numpy as jnp
from jax import lax
from jax.experimental import pallas as pl
from jax.experimental.pallas import tpu as pltpu
from jax.sharding import PartitionSpec as P


AXES = ("gx", "gy", "gz")
VM = pl.BlockSpec(memory_space=pltpu.VMEM)
SM = pl.BlockSpec(memory_space=pltpu.SMEM)
HB = pl.BlockSpec(memory_space=pltpu.HBM)
F32 = jnp.float32

NX, NY, NZ = 8, 32, 256
MX, MY, MZ = 4, 16, 128

X_LOW = [(c, x) for c in range(3) for x in range(-3 if c == 0 else -2, 0)]
X_HIGH = [(c, x) for c in range(3) for x in range(NX, NX + (4 if c == 0 else 2))]
NL, NH = len(X_LOW), len(X_HIGH)
PLANES = [(c, x) for c in range(3) for x in range(-3 if c == 0 else -2, NX + (4 if c == 0 else 2))]
PLANE_AT = {key: i for i, key in enumerate(PLANES)}
NP = len(PLANES)


def low_rows(c, x):
    inside = 0 <= x < NX
    if c == 0:
        return 2 if inside else (1 if x in (-1, NX, NX + 1) else 0)
    if c == 1:
        return 3 if inside else {-1: 1, NX: 2, NX + 1: 1}.get(x, 0)
    return 2 if inside else (1 if x in (-1, NX) else 0)


def high_rows(c, x):
    inside = 0 <= x < NX
    if c == 0:
        return 2 if inside or x in (-1, NX, NX + 1) else (1 if x in (-2, NX + 2) else 0)
    if c == 1:
        return 4 if inside else {-1: 2, NX: 3, NX + 1: 2}.get(x, 0)
    return 2 if inside else (1 if x in (-1, NX) else 0)


def row_table(count):
    table, at = [], 0
    for c, x in PLANES:
        n = count(c, x)
        if n:
            table.append((c, x, at, n))
            at += n
    return table, at


Y_LOW, Y_LOW_N = row_table(low_rows)
Y_HIGH, Y_HIGH_N = row_table(high_rows)
LOW_ZONES, HIGH_ZONES = 2 * Y_LOW_N, 2 * Y_HIGH_N
EX = 2 * (MX + 4)
Y_LOW_SIZE = -(-(LOW_ZONES + EX + MX) // 8) * 8
Y_HIGH_SIZE = -(-(HIGH_ZONES + EX + MX) // 8) * 8
Z_PLANES = [(c, x) for c, x in PLANES if -2 <= x <= NX + (2 if c == 0 else 1)]
ZN = len(Z_PLANES)
ZONE_SLOT = 2 * ZN
TRACER_SLOT = ZONE_SLOT + 2 * (MX + 4)
Z_TILES = -(-(TRACER_SLOT + MX) // 32)


def step_of(r):
    top = jnp.max(jnp.max(r[...], axis=0, keepdims=True), axis=1, keepdims=True)
    return 0.5 / jnp.sqrt(top)


def first_kernel(
    ratio, d, v, rho_in, energy_in, region_in, tracer_in,
    low, high, most, pressure, rho, tracer, energy, region, sems,
):
    copies = []

    def copy(src, dst):
        cp = pltpu.make_async_copy(src, dst, sems.at[len(copies)])
        cp.start()
        copies.append(cp)

    for pair in ((energy_in, energy), (region_in, region), (rho_in, rho), (tracer_in, tracer)):
        copy(*pair)
    for f, array in enumerate((d, v)):
        for c in range(3):
            n = 3 if c == 0 else 2
            copy(array.at[c, pl.ds(NX - n, n)], low.at[pl.ds(f * NL + X_LOW.index((c, -n)), n)])
            n = 4 if c == 0 else 2
            copy(array.at[c, pl.ds(0, n)], high.at[pl.ds(f * NH + X_HIGH.index((c, NX)), n)])
    for cp in copies[:4]:
        cp.wait()
    top = jnp.zeros((MY, MZ), F32)
    for i in range(MX):
        reg = region[i]
        zone_ratio = jnp.where(
            reg < 2,
            jnp.where(reg == 0, ratio[0], ratio[1]),
            jnp.where(reg == 2, ratio[2], ratio[3]),
        )
        pr = (zone_ratio - 1.0) * rho[i] * energy[i]
        pressure[i] = pr
        top = jnp.maximum(top, zone_ratio * (zone_ratio - 1.0) * energy[i])
        out, at = (high, 2 * NH) if i < 2 else (low, 2 * NL)
        lanes = slice(i % 2 * MZ, (i % 2 + 1) * MZ)
        out[at, :MY, lanes] = pr
        out[at, MY:, lanes] = rho[i]
    high[2 * NH + 1, :MY, :MZ] = tracer[0]
    low[2 * NL + 1, :MY, :MZ] = tracer[MX - 1]
    top = jnp.max(jnp.max(top, axis=0, keepdims=True), axis=1, keepdims=True)
    most[...] = jnp.broadcast_to(top, most.shape)
    for cp in copies[4:]:
        cp.wait()


def zone_plane(i, own, low, high, which):
    if 0 <= i < MX:
        return own[which][i]
    rows = pl.ds(which * MY, MY)
    if i < 0:
        return low[2 * NL, rows, (i + 2) * MZ : (i + 3) * MZ]
    return high[2 * NH, rows, (i - MX) * MZ : (i - MX + 1) * MZ]


def node_pair(c, x, d, v, low, high):
    if 0 <= x < NX:
        return d.at[c, x], v.at[c, x]
    if x < 0:
        i = X_LOW.index((c, x))
        return low.at[i], low.at[NL + i]
    i = X_HIGH.index((c, x))
    return high.at[i], high.at[NH + i]


def second_kernel(d, v, low, high, pressure, rho, tracer, ylow, yhigh):
    for table, size, out, top in ((Y_LOW, Y_LOW_N, ylow, True), (Y_HIGH, Y_HIGH_N, yhigh, False)):
        for c, x, at, n in table:
            first = NY - n if top else 0
            for f, plane in enumerate(node_pair(c, x, d, v, low, high)):
                out[pl.ds(f * size + at, n), :] = plane[pl.ds(first, n), :]
    for out, base, first, edge in ((ylow, LOW_ZONES, MY - 2, MY - 1), (yhigh, HIGH_ZONES, 0, 0)):
        for i in range(-2, MX + 2):
            for which in range(2):
                lanes = slice(which * MZ, (which + 1) * MZ)
                out[pl.ds(base + 2 * (i + 2), 2), lanes] = zone_plane(
                    i, (pressure, rho), low, high, which
                )[first : first + 2]
        for i in range(MX):
            out[pl.ds(base + EX + i, 1), :MZ] = tracer[i, pl.ds(edge, 1), :]


LOW_AT = {(c, x): (at, n) for c, x, at, n in Y_LOW}
HIGH_AT = {(c, x): (at, n) for c, x, at, n in Y_HIGH}


def zone_block(zones, pressure, rho, low, high, ylow, yhigh):
    for which in range(2):
        lanes = slice(which * MZ, (which + 1) * MZ)
        for i in range(-2, MX + 2):
            k = which * (MX + 4) + i + 2
            zones[k, pl.ds(4, MY), :MZ] = zone_plane(i, (pressure, rho), low, high, which)
            zones[k, pl.ds(2, 2), :MZ] = ylow[pl.ds(LOW_ZONES + 2 * (i + 2), 2), lanes]
            zones[k, pl.ds(4 + MY, 2), :MZ] = yhigh[pl.ds(HIGH_ZONES + 2 * (i + 2), 2), lanes]


def third_kernel(
    d, v, low, high, pressure, rho, tracer, ylow, yhigh, zlow, zhigh, zones, lefts, rights
):
    zone_block(zones, pressure, rho, low, high, ylow, yhigh)
    lane = lax.broadcasted_iota(jnp.int32, (1, 128), 1)
    for tile in range(Z_TILES):
        zlow[tile] = jnp.zeros((48, 128), F32)
        zhigh[tile] = jnp.zeros((48, 128), F32)
    for slot in range(TRACER_SLOT + MX):
        tile, s = divmod(slot, 32)
        here = (lane >= 4 * s) & (lane < 4 * s + 4)

        def put(rows, left, right):
            zhigh[tile, rows] = jnp.where(here, roll(left, 4 * s, 1), zhigh[tile, rows])
            zlow[tile, rows] = jnp.where(here, roll(right, 4 * s + 4, 1), zlow[tile, rows])

        if slot < ZONE_SLOT:
            f, e = divmod(slot, ZN)
            c, x = Z_PLANES[e]
            plane = node_pair(c, x, d, v, low, high)[f]
            put(pl.ds(8, NY), plane[:, :128], plane[:, 128:])
            if (c, x) in LOW_AT:
                at, n = LOW_AT[c, x]
                lefts[pl.ds(8 - n, n), :] = ylow[pl.ds(f * Y_LOW_N + at, n), :]
                put(pl.ds(0, 8), lefts[:, :128], lefts[:, 128:])
            if (c, x) in HIGH_AT:
                at, n = HIGH_AT[c, x]
                rights[pl.ds(0, n), :] = yhigh[pl.ds(f * Y_HIGH_N + at, n), :]
                put(pl.ds(8 + NY, 8), rights[:, :128], rights[:, 128:])
        elif slot < TRACER_SLOT:
            put(pl.ds(0, 24), zones[slot - ZONE_SLOT], zones[slot - ZONE_SLOT])
        else:
            put(pl.ds(0, MY), tracer[slot - TRACER_SLOT], tracer[slot - TRACER_SLOT])


def roll(value, by, axis):
    by %= value.shape[axis]
    return pltpu.roll(value, by, axis) if by else value


def pieces(value):
    first = value.astype(jnp.bfloat16)
    rest = value - first.astype(F32)
    second = rest.astype(jnp.bfloat16)
    return first, second, (rest - second.astype(F32)).astype(jnp.bfloat16)


def product(parts, matrix):
    total = None
    for part in parts:
        term = jnp.dot(part, matrix, preferred_element_type=F32)
        total = term if total is None else total + term
    return total


def last_kernel(
    r, d, v, low, high, pressure, rho, tracer, ylow, yhigh, zlow, zhigh,
    velocity, relaxed, remapped,
    moved, once, pz, qx, qy, qz, qm, moves, gathered, result, tz,
):
    step = step_of(r)
    lane = lax.broadcasted_iota(jnp.int32, (1, 128), 1)

    def beside(slot, n, fill):
        tile, s = divmod(slot, 32)
        rows = pl.ds(0, n)
        after = roll(zhigh[tile, rows], -4 * s, 1)
        before = roll(zlow[tile, rows], 124 - 4 * s, 1)
        return jnp.where(lane < 4, after, jnp.where(lane >= 124, before, fill))

    zone_block(pz, pressure, rho, low, high, ylow, yhigh)
    for k in range(2 * (MX + 4)):
        pz[k, :, MZ:] = beside(ZONE_SLOT + k, 24, 0.0 if k < MX + 4 else 1.0)
    k = lax.broadcasted_iota(jnp.int32, (2 * MZ, 384), 0)
    n = lax.broadcasted_iota(jnp.int32, (2 * MZ, 384), 1)
    a = jnp.where(n < 320, n, n - 384) - 2 * jnp.where(k < 192, k, k - 256)
    shape = jnp.where((a == 0) | (a == 2), 1.0, jnp.where(a == 1, 4.0, 0.0)).astype(jnp.bfloat16)
    slope = jnp.where(a == 0, -1.0, jnp.where(a == 2, 1.0, 0.0)).astype(jnp.bfloat16)
    half = (MX + 4) * 24
    both = pz[...].reshape(2 * half, 2 * MZ)
    spread = product(pieces(both), shape)
    slanted = product(pieces(both[:half]), slope)
    even, odd = pl.ds(0, 24, stride=2), pl.ds(1, 24, stride=2)

    def interleave(q, i, first, second):
        for t in range(3):
            lanes = slice(128 * t, 128 * t + 128)
            q[3 * i + t, even, :] = first[:, lanes]
            q[3 * i + t, odd, :] = second[:, lanes]

    def whole(q, i):
        return jnp.concatenate([q[3 * i + t] for t in range(3)], axis=1)

    for i in range(MX + 4):
        now = spread[24 * i : 24 * i + 24]
        before = roll(now, 1, 0)
        interleave(qx, i, now + before, 4.0 * now)
        interleave(qy, i, before - now, jnp.zeros((24, 384), F32))
        now = slanted[24 * i : 24 * i + 24]
        interleave(qz, i, now + roll(now, 1, 0), 4.0 * now)
        now = spread[half + 24 * i : half + 24 * i + 24]
        interleave(qm, i, now + roll(now, 1, 0), 4.0 * now)
    for x in range(-3, NX + 4):
        i = x // 2 + 2
        mass = whole(qm, i)
        mass = mass + whole(qm, i - 1) if x % 2 == 0 else 4.0 * mass
        push = 6.0 * step / mass
        for c in range(3):
            if (c, x) not in PLANE_AT:
                continue
            e = PLANE_AT[c, x]
            if c == 0:
                force = whole(qx, i - 1) - whole(qx, i) if x % 2 == 0 else None
            else:
                q = qy if c == 1 else qz
                force = whole(q, i)
                force = force + whole(q, i - 1) if x % 2 == 0 else 4.0 * force
            here, there = node_pair(c, x, d, v, low, high)
            moved[e, pl.ds(8, NY), :NZ] = here[...] + step * there[...]
            if (c, x) in LOW_AT:
                at, n = LOW_AT[c, x]
                moved[e, pl.ds(8 - n, n), :NZ] = (
                    ylow[pl.ds(at, n), :] + step * ylow[pl.ds(Y_LOW_N + at, n), :]
                )
            if (c, x) in HIGH_AT:
                at, n = HIGH_AT[c, x]
                moved[e, pl.ds(8 + NY, n), :NZ] = (
                    yhigh[pl.ds(at, n), :] + step * yhigh[pl.ds(Y_HIGH_N + at, n), :]
                )
            if (c, x) in Z_PLANES:
                z = Z_PLANES.index((c, x))
                moved[e, :, NZ:] = beside(z, 48, 0.0) + step * beside(ZN + z, 48, 0.0)
            else:
                moved[e, :, NZ:] = jnp.zeros((48, 128), F32)
            if force is not None:
                gain = force * push
                moved[e] = moved[e] + step * gain
            if 0 <= x < NX:
                new = v[c, x]
                velocity[c, x] = new if force is None else new + gain[8 : 8 + NY, :NZ]

    def sweep(ref, e, first, count, width):
        rows = pl.ds(first, count)
        now = ref[e, rows]
        sides = roll(now, 1, 1) + roll(now, -1, 1)
        rows_beside = ref[e, pl.ds(first - 1, count), :width] + ref[e, pl.ds(first + 1, count), :width]
        planes_beside = ref[e - 1, rows, :width] + ref[e + 1, rows, :width]
        total = planes_beside + rows_beside + sides[:, :width]
        return 0.1 * now[:, :width] + 0.15 * total

    for e, (c, x) in enumerate(PLANES):
        if (c, x - 1) in PLANE_AT and (c, x + 1) in PLANE_AT:
            now = moved[e]
            total = moved[e - 1] + moved[e + 1]
            total = total + (roll(now, 1, 0) + roll(now, -1, 0))
            total = total + (roll(now, 1, 1) + roll(now, -1, 1))
            once[e] = 0.1 * now + 0.15 * total
    at = 0
    for e, (c, x) in enumerate(PLANES):
        inside = 0 <= x < NX
        if not inside and not (c == 0 and x in (-1, NX + 1)):
            continue
        width = 384 if c == 2 and x % 2 else NZ
        if c == 1 and x % 2:
            edges = (sweep(once, e, 7, 1, width), sweep(once, e, 41, 1, width))
        twice = sweep(once, e, 8, NY, width)
        if inside:
            relaxed[c, x] = twice[:, :NZ]
        if x % 2:
            first, count = (7, 18) if c == 1 else (9, 16)
            for t in range(width // 128):
                lanes = slice(128 * t, 128 * t + 128)
                moves[t, pl.ds(8, NY), :] = twice[:, lanes] - moved[e, pl.ds(8, NY), lanes]
                if c == 1:
                    for row, edge in zip((7, 41), edges):
                        moves[t, pl.ds(row, 1), :] = edge[:, lanes] - moved[e, pl.ds(row, 1), lanes]
                gathered[pl.ds(at, count), lanes] = moves[t, pl.ds(first, count, stride=2), :]
            if c == 1:
                gathered[pl.ds(at + 18, 6), :] = jnp.zeros((6, 384), F32)
            at += 24 if c == 1 else 16
    gathered[pl.ds(0, (MX + 2) * 16 + MX * 24), NZ:] = jnp.zeros(((MX + 2) * 16 + MX * 24, 128), F32)
    n = lax.broadcasted_iota(jnp.int32, (384, 2 * MZ), 0)
    k = lax.broadcasted_iota(jnp.int32, (384, 2 * MZ), 1)
    node = jnp.where(n < 320, n, n - 384)
    chosen = (node == 2 * jnp.where(k < 192, k, k - 256) + 1).astype(F32).astype(jnp.bfloat16)
    result[...] = product(pieces(gathered[...]), chosen)

    def flux(speed, behind, here):
        donor = -(jnp.minimum(speed, 0.0) * behind + jnp.maximum(speed, 0.0) * here)
        return donor, -speed * 0.5 * (behind + here)

    y0, z0 = (MX + 2) * 16, (MX + 2) * 16 + MX * 24
    for i in range(MX):
        now = tracer[i]
        tz[pl.ds(8, MY), :] = now
        tz[pl.ds(7, 1), :] = ylow[pl.ds(LOW_ZONES + EX + i, 1), :MZ]
        tz[pl.ds(8 + MY, 1), :] = yhigh[pl.ds(HIGH_ZONES + EX + i, 1), :MZ]
        side = beside(TRACER_SLOT + i, MY, 0.0)
        edge = result[pl.ds(z0 + 16 * i, 16), MZ:]
        middle = result[pl.ds(z0 + 16 * i, 16), :MZ]
        around = (
            (
                tracer[i - 1] if i else low[2 * NL + 1, :MY, :MZ],
                tracer[i + 1] if i < MX - 1 else high[2 * NH + 1, :MY, :MZ],
                result[pl.ds(16 * i, 16), :MZ],
                result[pl.ds(16 * (i + 1), 16), :MZ],
                result[pl.ds(16 * (i + 2), 16), :MZ],
            ),
            (
                tz[pl.ds(7, MY), :],
                tz[pl.ds(9, MY), :],
                result[pl.ds(y0 + 24 * i, 16), :MZ],
                result[pl.ds(y0 + 24 * i + 1, 16), :MZ],
                result[pl.ds(y0 + 24 * i + 2, 16), :MZ],
            ),
            (
                jnp.where(lane == 0, roll(side, 1, 1), roll(now, 1, 1)),
                jnp.where(lane == MZ - 1, roll(side, -1, 1), roll(now, -1, 1)),
                jnp.where(lane == 0, roll(edge, 1, 1), roll(middle, 1, 1)),
                middle,
                jnp.where(lane == MZ - 1, roll(edge, -1, 1), roll(middle, -1, 1)),
            ),
        )
        donors = centrals = None
        floor = ceiling = now
        for behind, front, m0, m1, m2 in around:
            d0, c0 = flux(0.5 * (m0 + m1), behind, now)
            d1, c1 = flux(0.5 * (m1 + m2), now, front)
            donors = d1 - d0 if donors is None else donors + (d1 - d0)
            centrals = c1 - c0 if centrals is None else centrals + (c1 - c0)
            floor = jnp.minimum(jnp.minimum(floor, behind), front)
            ceiling = jnp.maximum(jnp.maximum(ceiling, behind), front)
        low_order = now - donors
        high_order = now - centrals
        floor = jnp.minimum(floor, low_order)
        ceiling = jnp.maximum(ceiling, low_order)
        remapped[i] = jnp.minimum(jnp.maximum(high_order, floor), ceiling)


def shape_of(*dims):
    return jax.ShapeDtypeStruct(dims, F32)


def local_of(*dims):
    return pltpu.VMEM(dims, F32)


def on_chip(array):
    return pltpu.with_memory_space_constraint(array, pltpu.VMEM)


def in_hbm(array):
    return pltpu.with_memory_space_constraint(array, pltpu.HBM)


def moved_along(block, axis, by):
    n = lax.axis_size(axis)
    return on_chip(lax.ppermute(block, axis, [(i, (i + by) % n) for i in range(n)]))


def pack_y(*operands):
    return pl.pallas_call(
        second_kernel,
        name="second",
        compiler_params=pltpu.CompilerParams(vmem_limit_bytes=8 << 20),
        in_specs=[VM] * 7,
        out_specs=[VM] * 2,
        out_shape=[local_of(Y_LOW_SIZE, NZ), local_of(Y_HIGH_SIZE, NZ)],
    )(*operands)


def on_device(displacement, velocity, density, energy, region, heat_ratio, tracer):
    n_devices = lax.axis_size(AXES)
    low, high, most, pressure, density, tracer = pl.pallas_call(
        first_kernel,
        name="first",
        compiler_params=pltpu.CompilerParams(vmem_limit_bytes=8 << 20),
        in_specs=[SM] + [HB] * 6,
        out_specs=[VM] * 6,
        out_shape=[
            local_of(2 * NL + 2, NY, NZ),
            local_of(2 * NH + 2, NY, NZ),
            local_of(n_devices, 128),
            local_of(MX, MY, MZ),
            local_of(MX, MY, MZ),
            local_of(MX, MY, MZ),
        ],
        scratch_shapes=[
            pltpu.VMEM((MX, MY, MZ), F32),
            pltpu.VMEM((MX, MY, MZ), jnp.int32),
            pltpu.SemaphoreType.DMA((16,)),
        ],
    )(*map(in_hbm, (heat_ratio, displacement, velocity, density, energy, region, tracer)))
    displacement, velocity = on_chip(displacement), on_chip(velocity)
    low = moved_along(low, "gx", 1)
    high = moved_along(high, "gx", -1)
    r = on_chip(lax.all_to_all(most, AXES, 0, 0, tiled=True))
    ylow, yhigh = pack_y(displacement, velocity, low, high, pressure, density, tracer)
    ylow = moved_along(ylow, "gy", 1)
    yhigh = moved_along(yhigh, "gy", -1)
    zlow, zhigh = pl.pallas_call(
        third_kernel,
        name="third",
        compiler_params=pltpu.CompilerParams(vmem_limit_bytes=8 << 20),
        in_specs=[VM] * 9,
        out_specs=[VM] * 2,
        out_shape=[local_of(Z_TILES, 48, 128)] * 2,
        scratch_shapes=[
            pltpu.VMEM((2 * (MX + 4), 24, MZ), F32),
            pltpu.VMEM((8, NZ), F32),
            pltpu.VMEM((8, NZ), F32),
        ],
    )(displacement, velocity, low, high, pressure, density, tracer, ylow, yhigh)
    zlow = moved_along(zlow, "gz", 1)
    zhigh = moved_along(zhigh, "gz", -1)
    q = pltpu.VMEM((3 * (MX + 4), 48, 128), F32)
    return pl.pallas_call(
        last_kernel,
        name="last",
        compiler_params=pltpu.CompilerParams(vmem_limit_bytes=30 << 20),
        in_specs=[VM] * 12,
        out_specs=[VM] * 3,
        out_shape=[shape_of(3, NX, NY, NZ), shape_of(3, NX, NY, NZ), shape_of(MX, MY, MZ)],
        scratch_shapes=[
            pltpu.VMEM((NP, 48, 384), F32),
            pltpu.VMEM((NP, 48, 384), F32),
            pltpu.VMEM((2 * (MX + 4), 24, 2 * MZ), F32),
            q, q, q, q,
            pltpu.VMEM((3, 48, 128), F32),
            pltpu.VMEM((256, 384), F32),
            pltpu.VMEM((256, 2 * MZ), F32),
            pltpu.VMEM((MY + 16, MZ), F32),
        ],
    )(
        r, displacement, velocity, low, high, pressure, density, tracer, ylow, yhigh, zlow, zhigh
    )


def solution(mesh):
    node, zone = P(None, "gx", "gy", "gz"), P("gx", "gy", "gz")
    return jax.shard_map(
        on_device,
        mesh=mesh,
        in_specs=(node, node, zone, zone, zone, P(), zone),
        out_specs=(node, node, zone),
        check_vma=False,
    )
```

```python
import jax
import jax.numpy as jnp
from jax import lax
from jax.experimental import pallas as pl
from jax.experimental.pallas import tpu as pltpu
from jax.sharding import PartitionSpec as P


PEERS = ("gy", "gz")
VM = pl.BlockSpec(memory_space=pltpu.VMEM)
SM = pl.BlockSpec(memory_space=pltpu.SMEM)
HB = pl.BlockSpec(memory_space=pltpu.HBM)
F32 = jnp.float32

NX, NY, NZ = 8, 32, 256
MX, MY, MZ = 4, 16, 128

X_LOW = [(c, x) for c in range(3) for x in range(-3 if c == 0 else -2, 0)]
X_HIGH = [(c, x) for c in range(3) for x in range(NX, NX + (4 if c == 0 else 2))]
NL, NH = len(X_LOW), len(X_HIGH)
PLANES = [(c, x) for c in range(3) for x in range(-3 if c == 0 else -2, NX + (4 if c == 0 else 2))]
PLANE_AT = {key: i for i, key in enumerate(PLANES)}
NP = len(PLANES)


def low_rows(c, x):
    inside = 0 <= x < NX
    if c == 0:
        return 2 if inside else (1 if x in (-1, NX, NX + 1) else 0)
    if c == 1:
        return 3 if inside else {-1: 1, NX: 2, NX + 1: 1}.get(x, 0)
    return 2 if inside else (1 if x in (-1, NX) else 0)


def high_rows(c, x):
    inside = 0 <= x < NX
    if c == 0:
        return 2 if inside or x in (-1, NX, NX + 1) else (1 if x in (-2, NX + 2) else 0)
    if c == 1:
        return 4 if inside else {-1: 2, NX: 3, NX + 1: 2}.get(x, 0)
    return 2 if inside else (1 if x in (-1, NX) else 0)


def row_table(count):
    table, at = [], 0
    for c, x in PLANES:
        n = count(c, x)
        if n:
            table.append((c, x, at, n))
            at += n
    return table, at


Y_LOW, Y_LOW_N = row_table(low_rows)
Y_HIGH, Y_HIGH_N = row_table(high_rows)
LOW_ZONES, HIGH_ZONES = 2 * Y_LOW_N, 2 * Y_HIGH_N
EX = 2 * (MX + 4)
Y_LOW_SIZE = -(-(LOW_ZONES + EX + MX) // 8) * 8
Y_HIGH_SIZE = -(-(HIGH_ZONES + EX + MX) // 8) * 8
Z_PLANES = [(c, x) for c, x in PLANES if -2 <= x <= NX + (2 if c == 0 else 1)]
ZN = len(Z_PLANES)
ZONE_SLOT = 2 * ZN
TRACER_SLOT = ZONE_SLOT + 2 * (MX + 4)
Z_TILES = -(-(TRACER_SLOT + MX) // 32)


def step_of(tops):
    r = tops[0][...]
    for other in tops[1:]:
        r = jnp.maximum(r, other[...])
    top = jnp.max(jnp.max(r, axis=0, keepdims=True), axis=1, keepdims=True)
    return 0.5 / jnp.sqrt(top)


def first_kernel(
    ratio, d, v, rho_in, energy_in, region_in, tracer_in,
    low, high, most, pressure, rho, tracer, energy, region, sems,
):
    copies = []

    def copy(src, dst):
        cp = pltpu.make_async_copy(src, dst, sems.at[len(copies)])
        cp.start()
        copies.append(cp)

    for pair in ((energy_in, energy), (region_in, region), (rho_in, rho), (tracer_in, tracer)):
        copy(*pair)
    for f, array in enumerate((d, v)):
        for c in range(3):
            n = 3 if c == 0 else 2
            copy(array.at[c, pl.ds(NX - n, n)], low.at[pl.ds(f * NL + X_LOW.index((c, -n)), n)])
            n = 4 if c == 0 else 2
            copy(array.at[c, pl.ds(0, n)], high.at[pl.ds(f * NH + X_HIGH.index((c, NX)), n)])
    for cp in copies[:4]:
        cp.wait()
    top = jnp.zeros((MY, MZ), F32)
    for i in range(MX):
        reg = region[i]
        zone_ratio = jnp.where(
            reg < 2,
            jnp.where(reg == 0, ratio[0], ratio[1]),
            jnp.where(reg == 2, ratio[2], ratio[3]),
        )
        pr = (zone_ratio - 1.0) * rho[i] * energy[i]
        pressure[i] = pr
        top = jnp.maximum(top, zone_ratio * (zone_ratio - 1.0) * energy[i])
        out, at = (high, 2 * NH) if i < 2 else (low, 2 * NL)
        lanes = slice(i % 2 * MZ, (i % 2 + 1) * MZ)
        out[at, :MY, lanes] = pr
        out[at, MY:, lanes] = rho[i]
    high[2 * NH + 1, :MY, :MZ] = tracer[0]
    low[2 * NL + 1, :MY, :MZ] = tracer[MX - 1]
    top = jnp.max(jnp.max(top, axis=0, keepdims=True), axis=1, keepdims=True)
    most[...] = jnp.broadcast_to(top, most.shape)
    for cp in copies[4:]:
        cp.wait()


def zone_plane(i, own, low, high, which):
    if 0 <= i < MX:
        return own[which][i]
    rows = pl.ds(which * MY, MY)
    if i < 0:
        return low[2 * NL, rows, (i + 2) * MZ : (i + 3) * MZ]
    return high[2 * NH, rows, (i - MX) * MZ : (i - MX + 1) * MZ]


def node_pair(c, x, d, v, low, high):
    if 0 <= x < NX:
        return d.at[c, x], v.at[c, x]
    if x < 0:
        i = X_LOW.index((c, x))
        return low.at[i], low.at[NL + i]
    i = X_HIGH.index((c, x))
    return high.at[i], high.at[NH + i]


def second_kernel(d, v, low, high, pressure, rho, tracer, ylow, yhigh):
    for table, size, out, top in ((Y_LOW, Y_LOW_N, ylow, True), (Y_HIGH, Y_HIGH_N, yhigh, False)):
        for c, x, at, n in table:
            first = NY - n if top else 0
            for f, plane in enumerate(node_pair(c, x, d, v, low, high)):
                out[pl.ds(f * size + at, n), :] = plane[pl.ds(first, n), :]
    for out, base, first, edge in ((ylow, LOW_ZONES, MY - 2, MY - 1), (yhigh, HIGH_ZONES, 0, 0)):
        for i in range(-2, MX + 2):
            for which in range(2):
                lanes = slice(which * MZ, (which + 1) * MZ)
                out[pl.ds(base + 2 * (i + 2), 2), lanes] = zone_plane(
                    i, (pressure, rho), low, high, which
                )[first : first + 2]
        for i in range(MX):
            out[pl.ds(base + EX + i, 1), :MZ] = tracer[i, pl.ds(edge, 1), :]


LOW_AT = {(c, x): (at, n) for c, x, at, n in Y_LOW}
HIGH_AT = {(c, x): (at, n) for c, x, at, n in Y_HIGH}


def zone_block(zones, pressure, rho, low, high, ylow, yhigh):
    for which in range(2):
        lanes = slice(which * MZ, (which + 1) * MZ)
        for i in range(-2, MX + 2):
            k = which * (MX + 4) + i + 2
            zones[k, pl.ds(4, MY), :MZ] = zone_plane(i, (pressure, rho), low, high, which)
            zones[k, pl.ds(2, 2), :MZ] = ylow[pl.ds(LOW_ZONES + 2 * (i + 2), 2), lanes]
            zones[k, pl.ds(4 + MY, 2), :MZ] = yhigh[pl.ds(HIGH_ZONES + 2 * (i + 2), 2), lanes]


def third_kernel(
    d, v, low, high, pressure, rho, tracer, ylow, yhigh, zlow, zhigh, zones, lefts, rights
):
    zone_block(zones, pressure, rho, low, high, ylow, yhigh)
    lane = lax.broadcasted_iota(jnp.int32, (1, 128), 1)
    for tile in range(Z_TILES):
        zlow[tile] = jnp.zeros((48, 128), F32)
        zhigh[tile] = jnp.zeros((48, 128), F32)
    for slot in range(TRACER_SLOT + MX):
        tile, s = divmod(slot, 32)
        here = (lane >= 4 * s) & (lane < 4 * s + 4)

        def put(rows, left, right):
            zhigh[tile, rows] = jnp.where(here, roll(left, 4 * s, 1), zhigh[tile, rows])
            zlow[tile, rows] = jnp.where(here, roll(right, 4 * s + 4, 1), zlow[tile, rows])

        if slot < ZONE_SLOT:
            f, e = divmod(slot, ZN)
            c, x = Z_PLANES[e]
            plane = node_pair(c, x, d, v, low, high)[f]
            put(pl.ds(8, NY), plane[:, :128], plane[:, 128:])
            if (c, x) in LOW_AT:
                at, n = LOW_AT[c, x]
                lefts[pl.ds(8 - n, n), :] = ylow[pl.ds(f * Y_LOW_N + at, n), :]
                put(pl.ds(0, 8), lefts[:, :128], lefts[:, 128:])
            if (c, x) in HIGH_AT:
                at, n = HIGH_AT[c, x]
                rights[pl.ds(0, n), :] = yhigh[pl.ds(f * Y_HIGH_N + at, n), :]
                put(pl.ds(8 + NY, 8), rights[:, :128], rights[:, 128:])
        elif slot < TRACER_SLOT:
            put(pl.ds(0, 24), zones[slot - ZONE_SLOT], zones[slot - ZONE_SLOT])
        else:
            put(pl.ds(0, MY), tracer[slot - TRACER_SLOT], tracer[slot - TRACER_SLOT])


def roll(value, by, axis):
    by %= value.shape[axis]
    return pltpu.roll(value, by, axis) if by else value


def pieces(value):
    first = value.astype(jnp.bfloat16)
    rest = value - first.astype(F32)
    second = rest.astype(jnp.bfloat16)
    return first, second, (rest - second.astype(F32)).astype(jnp.bfloat16)


def product(parts, matrix):
    total = None
    for part in parts:
        term = jnp.dot(part, matrix, preferred_element_type=F32)
        total = term if total is None else total + term
    return total


def last_kernel(
    r0, r1, r2, r3, d, v, low, high, pressure, rho, tracer, ylow, yhigh, zlow, zhigh,
    velocity, relaxed, remapped,
    moved, once, pz, qx, qy, qz, qm, moves, gathered, result, tz,
):
    step = step_of((r0, r1, r2, r3))
    lane = lax.broadcasted_iota(jnp.int32, (1, 128), 1)

    def beside(slot, n, fill):
        tile, s = divmod(slot, 32)
        rows = pl.ds(0, n)
        after = roll(zhigh[tile, rows], -4 * s, 1)
        before = roll(zlow[tile, rows], 124 - 4 * s, 1)
        return jnp.where(lane < 4, after, jnp.where(lane >= 124, before, fill))

    zone_block(pz, pressure, rho, low, high, ylow, yhigh)
    for k in range(2 * (MX + 4)):
        pz[k, :, MZ:] = beside(ZONE_SLOT + k, 24, 0.0 if k < MX + 4 else 1.0)
    k = lax.broadcasted_iota(jnp.int32, (2 * MZ, 384), 0)
    n = lax.broadcasted_iota(jnp.int32, (2 * MZ, 384), 1)
    a = jnp.where(n < 320, n, n - 384) - 2 * jnp.where(k < 192, k, k - 256)
    shape = jnp.where((a == 0) | (a == 2), 1.0, jnp.where(a == 1, 4.0, 0.0)).astype(jnp.bfloat16)
    slope = jnp.where(a == 0, -1.0, jnp.where(a == 2, 1.0, 0.0)).astype(jnp.bfloat16)
    half = (MX + 4) * 24
    both = pz[...].reshape(2 * half, 2 * MZ)
    spread = product(pieces(both), shape)
    slanted = product(pieces(both[:half]), slope)
    even, odd = pl.ds(0, 24, stride=2), pl.ds(1, 24, stride=2)

    def interleave(q, i, first, second):
        for t in range(3):
            lanes = slice(128 * t, 128 * t + 128)
            q[3 * i + t, even, :] = first[:, lanes]
            q[3 * i + t, odd, :] = second[:, lanes]

    def whole(q, i):
        return jnp.concatenate([q[3 * i + t] for t in range(3)], axis=1)

    for i in range(MX + 4):
        now = spread[24 * i : 24 * i + 24]
        before = roll(now, 1, 0)
        interleave(qx, i, now + before, 4.0 * now)
        interleave(qy, i, before - now, jnp.zeros((24, 384), F32))
        now = slanted[24 * i : 24 * i + 24]
        interleave(qz, i, now + roll(now, 1, 0), 4.0 * now)
        now = spread[half + 24 * i : half + 24 * i + 24]
        interleave(qm, i, now + roll(now, 1, 0), 4.0 * now)
    for x in range(-3, NX + 4):
        i = x // 2 + 2
        mass = whole(qm, i)
        mass = mass + whole(qm, i - 1) if x % 2 == 0 else 4.0 * mass
        push = 6.0 * step / mass
        for c in range(3):
            if (c, x) not in PLANE_AT:
                continue
            e = PLANE_AT[c, x]
            if c == 0:
                force = whole(qx, i - 1) - whole(qx, i) if x % 2 == 0 else None
            else:
                q = qy if c == 1 else qz
                force = whole(q, i)
                force = force + whole(q, i - 1) if x % 2 == 0 else 4.0 * force
            here, there = node_pair(c, x, d, v, low, high)
            moved[e, pl.ds(8, NY), :NZ] = here[...] + step * there[...]
            if (c, x) in LOW_AT:
                at, n = LOW_AT[c, x]
                moved[e, pl.ds(8 - n, n), :NZ] = (
                    ylow[pl.ds(at, n), :] + step * ylow[pl.ds(Y_LOW_N + at, n), :]
                )
            if (c, x) in HIGH_AT:
                at, n = HIGH_AT[c, x]
                moved[e, pl.ds(8 + NY, n), :NZ] = (
                    yhigh[pl.ds(at, n), :] + step * yhigh[pl.ds(Y_HIGH_N + at, n), :]
                )
            if (c, x) in Z_PLANES:
                z = Z_PLANES.index((c, x))
                moved[e, :, NZ:] = beside(z, 48, 0.0) + step * beside(ZN + z, 48, 0.0)
            else:
                moved[e, :, NZ:] = jnp.zeros((48, 128), F32)
            if force is not None:
                gain = force * push
                moved[e] = moved[e] + step * gain
            if 0 <= x < NX:
                new = v[c, x]
                velocity[c, x] = new if force is None else new + gain[8 : 8 + NY, :NZ]

    def sweep(ref, e, first, count, width):
        rows = pl.ds(first, count)
        now = ref[e, rows]
        sides = roll(now, 1, 1) + roll(now, -1, 1)
        rows_beside = ref[e, pl.ds(first - 1, count), :width] + ref[e, pl.ds(first + 1, count), :width]
        planes_beside = ref[e - 1, rows, :width] + ref[e + 1, rows, :width]
        total = planes_beside + rows_beside + sides[:, :width]
        return 0.1 * now[:, :width] + 0.15 * total

    for e, (c, x) in enumerate(PLANES):
        if (c, x - 1) in PLANE_AT and (c, x + 1) in PLANE_AT:
            now = moved[e]
            total = moved[e - 1] + moved[e + 1]
            total = total + (roll(now, 1, 0) + roll(now, -1, 0))
            total = total + (roll(now, 1, 1) + roll(now, -1, 1))
            once[e] = 0.1 * now + 0.15 * total
    at = 0
    for e, (c, x) in enumerate(PLANES):
        inside = 0 <= x < NX
        if not inside and not (c == 0 and x in (-1, NX + 1)):
            continue
        width = 384 if c == 2 and x % 2 else NZ
        if c == 1 and x % 2:
            edges = (sweep(once, e, 7, 1, width), sweep(once, e, 41, 1, width))
        twice = sweep(once, e, 8, NY, width)
        if inside:
            relaxed[c, x] = twice[:, :NZ]
        if x % 2:
            first, count = (7, 18) if c == 1 else (9, 16)
            for t in range(width // 128):
                lanes = slice(128 * t, 128 * t + 128)
                moves[t, pl.ds(8, NY), :] = twice[:, lanes] - moved[e, pl.ds(8, NY), lanes]
                if c == 1:
                    for row, edge in zip((7, 41), edges):
                        moves[t, pl.ds(row, 1), :] = edge[:, lanes] - moved[e, pl.ds(row, 1), lanes]
                gathered[pl.ds(at, count), lanes] = moves[t, pl.ds(first, count, stride=2), :]
            if c == 1:
                gathered[pl.ds(at + 18, 6), :] = jnp.zeros((6, 384), F32)
            at += 24 if c == 1 else 16
    gathered[pl.ds(0, (MX + 2) * 16 + MX * 24), NZ:] = jnp.zeros(((MX + 2) * 16 + MX * 24, 128), F32)
    n = lax.broadcasted_iota(jnp.int32, (384, 2 * MZ), 0)
    k = lax.broadcasted_iota(jnp.int32, (384, 2 * MZ), 1)
    node = jnp.where(n < 320, n, n - 384)
    chosen = (node == 2 * jnp.where(k < 192, k, k - 256) + 1).astype(F32).astype(jnp.bfloat16)
    result[...] = product(pieces(gathered[...]), chosen)

    def flux(speed, behind, here):
        donor = -(jnp.minimum(speed, 0.0) * behind + jnp.maximum(speed, 0.0) * here)
        return donor, -speed * 0.5 * (behind + here)

    y0, z0 = (MX + 2) * 16, (MX + 2) * 16 + MX * 24
    for i in range(MX):
        now = tracer[i]
        tz[pl.ds(8, MY), :] = now
        tz[pl.ds(7, 1), :] = ylow[pl.ds(LOW_ZONES + EX + i, 1), :MZ]
        tz[pl.ds(8 + MY, 1), :] = yhigh[pl.ds(HIGH_ZONES + EX + i, 1), :MZ]
        side = beside(TRACER_SLOT + i, MY, 0.0)
        edge = result[pl.ds(z0 + 16 * i, 16), MZ:]
        middle = result[pl.ds(z0 + 16 * i, 16), :MZ]
        around = (
            (
                tracer[i - 1] if i else low[2 * NL + 1, :MY, :MZ],
                tracer[i + 1] if i < MX - 1 else high[2 * NH + 1, :MY, :MZ],
                result[pl.ds(16 * i, 16), :MZ],
                result[pl.ds(16 * (i + 1), 16), :MZ],
                result[pl.ds(16 * (i + 2), 16), :MZ],
            ),
            (
                tz[pl.ds(7, MY), :],
                tz[pl.ds(9, MY), :],
                result[pl.ds(y0 + 24 * i, 16), :MZ],
                result[pl.ds(y0 + 24 * i + 1, 16), :MZ],
                result[pl.ds(y0 + 24 * i + 2, 16), :MZ],
            ),
            (
                jnp.where(lane == 0, roll(side, 1, 1), roll(now, 1, 1)),
                jnp.where(lane == MZ - 1, roll(side, -1, 1), roll(now, -1, 1)),
                jnp.where(lane == 0, roll(edge, 1, 1), roll(middle, 1, 1)),
                middle,
                jnp.where(lane == MZ - 1, roll(edge, -1, 1), roll(middle, -1, 1)),
            ),
        )
        donors = centrals = None
        floor = ceiling = now
        for behind, front, m0, m1, m2 in around:
            d0, c0 = flux(0.5 * (m0 + m1), behind, now)
            d1, c1 = flux(0.5 * (m1 + m2), now, front)
            donors = d1 - d0 if donors is None else donors + (d1 - d0)
            centrals = c1 - c0 if centrals is None else centrals + (c1 - c0)
            floor = jnp.minimum(jnp.minimum(floor, behind), front)
            ceiling = jnp.maximum(jnp.maximum(ceiling, behind), front)
        low_order = now - donors
        high_order = now - centrals
        floor = jnp.minimum(floor, low_order)
        ceiling = jnp.maximum(ceiling, low_order)
        remapped[i] = jnp.minimum(jnp.maximum(high_order, floor), ceiling)


def shape_of(*dims):
    return jax.ShapeDtypeStruct(dims, F32)


def local_of(*dims):
    return pltpu.VMEM(dims, F32)


def on_chip(array):
    return pltpu.with_memory_space_constraint(array, pltpu.VMEM)


def in_hbm(array):
    return pltpu.with_memory_space_constraint(array, pltpu.HBM)


def moved_along(block, axis, by):
    n = lax.axis_size(axis)
    return on_chip(lax.ppermute(block, axis, [(i, (i + by) % n) for i in range(n)]))


def pack_y(*operands):
    return pl.pallas_call(
        second_kernel,
        name="second",
        compiler_params=pltpu.CompilerParams(vmem_limit_bytes=8 << 20),
        in_specs=[VM] * 7,
        out_specs=[VM] * 2,
        out_shape=[local_of(Y_LOW_SIZE, NZ), local_of(Y_HIGH_SIZE, NZ)],
    )(*operands)


def on_device(displacement, velocity, density, energy, region, heat_ratio, tracer):
    n_peers = lax.axis_size(PEERS)
    low, high, most, pressure, density, tracer = pl.pallas_call(
        first_kernel,
        name="first",
        compiler_params=pltpu.CompilerParams(vmem_limit_bytes=8 << 20),
        in_specs=[SM] + [HB] * 6,
        out_specs=[VM] * 6,
        out_shape=[
            local_of(2 * NL + 2, NY, NZ),
            local_of(2 * NH + 2, NY, NZ),
            local_of(n_peers, 128),
            local_of(MX, MY, MZ),
            local_of(MX, MY, MZ),
            local_of(MX, MY, MZ),
        ],
        scratch_shapes=[
            pltpu.VMEM((MX, MY, MZ), F32),
            pltpu.VMEM((MX, MY, MZ), jnp.int32),
            pltpu.SemaphoreType.DMA((16,)),
        ],
    )(*map(in_hbm, (heat_ratio, displacement, velocity, density, energy, region, tracer)))
    displacement, velocity = on_chip(displacement), on_chip(velocity)
    low = moved_along(low, "gx", 1)
    high = moved_along(high, "gx", -1)
    r = on_chip(lax.all_to_all(most, PEERS, 0, 0, tiled=True))
    ylow, yhigh = pack_y(displacement, velocity, low, high, pressure, density, tracer)
    ylow = moved_along(ylow, "gy", 1)
    yhigh = moved_along(yhigh, "gy", -1)
    zlow, zhigh = pl.pallas_call(
        third_kernel,
        name="third",
        compiler_params=pltpu.CompilerParams(vmem_limit_bytes=8 << 20),
        in_specs=[VM] * 9,
        out_specs=[VM] * 2,
        out_shape=[local_of(Z_TILES, 48, 128)] * 2,
        scratch_shapes=[
            pltpu.VMEM((2 * (MX + 4), 24, MZ), F32),
            pltpu.VMEM((8, NZ), F32),
            pltpu.VMEM((8, NZ), F32),
        ],
    )(displacement, velocity, low, high, pressure, density, tracer, ylow, yhigh)
    zlow = moved_along(zlow, "gz", 1)
    zhigh = moved_along(zhigh, "gz", -1)
    tops = [r]
    for by in (1, -1, 2):
        tops.append(moved_along(r, "gx", by))
    q = pltpu.VMEM((3 * (MX + 4), 48, 128), F32)
    return pl.pallas_call(
        last_kernel,
        name="last",
        compiler_params=pltpu.CompilerParams(vmem_limit_bytes=30 << 20),
        in_specs=[VM] * 15,
        out_specs=[VM] * 3,
        out_shape=[shape_of(3, NX, NY, NZ), shape_of(3, NX, NY, NZ), shape_of(MX, MY, MZ)],
        scratch_shapes=[
            pltpu.VMEM((NP, 48, 384), F32),
            pltpu.VMEM((NP, 48, 384), F32),
            pltpu.VMEM((2 * (MX + 4), 24, 2 * MZ), F32),
            q, q, q, q,
            pltpu.VMEM((3, 48, 128), F32),
            pltpu.VMEM((256, 384), F32),
            pltpu.VMEM((256, 2 * MZ), F32),
            pltpu.VMEM((MY + 16, MZ), F32),
        ],
    )(
        *tops, displacement, velocity, low, high, pressure, density, tracer, ylow, yhigh, zlow, zhigh
    )


def solution(mesh):
    node, zone = P(None, "gx", "gy", "gz"), P("gx", "gy", "gz")
    return jax.shard_map(
        on_device,
        mesh=mesh,
        in_specs=(node, node, zone, zone, zone, P(), zone),
        out_specs=(node, node, zone),
        check_vma=False,
    )
```

```python
import jax
import jax.numpy as jnp
from jax import lax
from jax.experimental import pallas as pl
from jax.experimental.pallas import tpu as pltpu
from jax.sharding import PartitionSpec as P


AXES = ("gx", "gy", "gz")
VM = pl.BlockSpec(memory_space=pltpu.VMEM)
SM = pl.BlockSpec(memory_space=pltpu.SMEM)
HB = pl.BlockSpec(memory_space=pltpu.HBM)
F32 = jnp.float32

NX, NY, NZ = 8, 32, 256
MX, MY, MZ = 4, 16, 128

X_LOW = [(c, x) for c in range(3) for x in range(-3 if c == 0 else -2, 0)]
X_HIGH = [(c, x) for c in range(3) for x in range(NX, NX + (4 if c == 0 else 2))]
NL, NH = len(X_LOW), len(X_HIGH)
PLANES = [(c, x) for c in range(3) for x in range(-3 if c == 0 else -2, NX + (4 if c == 0 else 2))]
PLANE_AT = {key: i for i, key in enumerate(PLANES)}
NP = len(PLANES)


def low_rows(c, x):
    inside = 0 <= x < NX
    if c == 0:
        return 2 if inside else (1 if x in (-1, NX, NX + 1) else 0)
    if c == 1:
        return 3 if inside else {-1: 1, NX: 2, NX + 1: 1}.get(x, 0)
    return 2 if inside else (1 if x in (-1, NX) else 0)


def high_rows(c, x):
    inside = 0 <= x < NX
    if c == 0:
        return 2 if inside or x in (-1, NX, NX + 1) else (1 if x in (-2, NX + 2) else 0)
    if c == 1:
        return 4 if inside else {-1: 2, NX: 3, NX + 1: 2}.get(x, 0)
    return 2 if inside else (1 if x in (-1, NX) else 0)


def row_tables(count):
    tables, sizes = ([], []), [0, 0]
    for c, x in PLANES:
        n, part = count(c, x), 0 if 0 <= x < NX else 1
        if n:
            tables[part].append((c, x, sizes[part], n))
            sizes[part] += n
    return tables, sizes


Y_LOW, Y_LOW_N = row_tables(low_rows)
Y_HIGH, Y_HIGH_N = row_tables(high_rows)
ZONE_ROWS = (3 * MX, 8)


def buffer_rows(sizes, part):
    return -(-(2 * sizes[part] + ZONE_ROWS[part]) // 8) * 8


Z_PLANES = [(c, x) for c, x in PLANES if -2 <= x <= NX + (2 if c == 0 else 1)]
ZN = len(Z_PLANES)
ZONE_SLOT = 2 * ZN
TRACER_SLOT = ZONE_SLOT + 2 * (MX + 4)
Z_TILES = -(-(TRACER_SLOT + MX) // 32)


def step_of(r):
    top = jnp.max(jnp.max(r[...], axis=0, keepdims=True), axis=1, keepdims=True)
    return 0.5 / jnp.sqrt(top)


def first_kernel(
    ratio, d, v, rho_in, energy_in, region_in, tracer_in,
    low, high, most, pressure, rho, tracer, ylow, yhigh, energy, region, ends, starts, sems,
):
    copies = []

    def copy(src, dst):
        cp = pltpu.make_async_copy(src, dst, sems.at[len(copies)])
        cp.start()
        copies.append(cp)

    for pair in ((energy_in, energy), (region_in, region), (rho_in, rho), (tracer_in, tracer)):
        copy(*pair)
    for f, array in enumerate((d, v)):
        copy(array.at[:, :, pl.ds(NY - 8, 8)], ends.at[f])
        copy(array.at[:, :, pl.ds(0, 8)], starts.at[f])
    for f, array in enumerate((d, v)):
        for c in range(3):
            n = 3 if c == 0 else 2
            copy(array.at[c, pl.ds(NX - n, n)], low.at[pl.ds(f * NL + X_LOW.index((c, -n)), n)])
            n = 4 if c == 0 else 2
            copy(array.at[c, pl.ds(0, n)], high.at[pl.ds(f * NH + X_HIGH.index((c, NX)), n)])
    for cp in copies[:4]:
        cp.wait()
    top = jnp.zeros((MY, MZ), F32)
    for i in range(MX):
        reg = region[i]
        zone_ratio = jnp.where(
            reg < 2,
            jnp.where(reg == 0, ratio[0], ratio[1]),
            jnp.where(reg == 2, ratio[2], ratio[3]),
        )
        pr = (zone_ratio - 1.0) * rho[i] * energy[i]
        pressure[i] = pr
        top = jnp.maximum(top, zone_ratio * (zone_ratio - 1.0) * energy[i])
        out, at = (high, 2 * NH) if i < 2 else (low, 2 * NL)
        lanes = slice(i % 2 * MZ, (i % 2 + 1) * MZ)
        out[at, :MY, lanes] = pr
        out[at, MY:, lanes] = rho[i]
    high[2 * NH + 1, :MY, :MZ] = tracer[0]
    low[2 * NL + 1, :MY, :MZ] = tracer[MX - 1]
    top = jnp.max(jnp.max(top, axis=0, keepdims=True), axis=1, keepdims=True)
    most[...] = jnp.broadcast_to(top, most.shape)
    for cp in copies[4:8]:
        cp.wait()
    for (table, _), sizes, out, rows, zone, edge in (
        (Y_LOW, Y_LOW_N, ylow, ends, MY - 2, MY - 1),
        (Y_HIGH, Y_HIGH_N, yhigh, starts, 0, 0),
    ):
        for c, x, at, n in table:
            for f in range(2):
                first = 8 - n if edge else 0
                out[pl.ds(f * sizes[0] + at, n), :] = rows[f, c, x, pl.ds(first, n), :]
        for i in range(MX):
            at = pl.ds(2 * sizes[0] + 2 * i, 2)
            out[at, :MZ] = pressure[i, pl.ds(zone, 2), :]
            out[at, MZ:] = rho[i, pl.ds(zone, 2), :]
            out[pl.ds(2 * sizes[0] + 2 * MX + i, 1), :MZ] = tracer[i, pl.ds(edge, 1), :]
    for cp in copies[8:]:
        cp.wait()


def zone_plane(i, own, low, high, which):
    if 0 <= i < MX:
        return own[which][i]
    rows = pl.ds(which * MY, MY)
    if i < 0:
        return low[2 * NL, rows, (i + 2) * MZ : (i + 3) * MZ]
    return high[2 * NH, rows, (i - MX) * MZ : (i - MX + 1) * MZ]


def node_pair(c, x, d, v, low, high):
    if 0 <= x < NX:
        return d.at[c, x], v.at[c, x]
    if x < 0:
        i = X_LOW.index((c, x))
        return low.at[i], low.at[NL + i]
    i = X_HIGH.index((c, x))
    return high.at[i], high.at[NH + i]


def second_kernel(low, high, ylow, yhigh):
    for (_, table), sizes, out, is_low in (
        (Y_LOW, Y_LOW_N, ylow, True),
        (Y_HIGH, Y_HIGH_N, yhigh, False),
    ):
        for c, x, at, n in table:
            first = NY - n if is_low else 0
            for f, plane in enumerate(node_pair(c, x, None, None, low, high)):
                out[pl.ds(f * sizes[1] + at, n), :] = plane[pl.ds(first, n), :]
        first = MY - 2 if is_low else 0
        for k, i in enumerate((-2, -1, MX, MX + 1)):
            for which in range(2):
                lanes = slice(which * MZ, (which + 1) * MZ)
                rows = zone_plane(i, None, low, high, which)[first : first + 2]
                out[pl.ds(2 * sizes[1] + 2 * k, 2), lanes] = rows


def places(tables):
    return {(c, x): (part, at, n) for part in (0, 1) for c, x, at, n in tables[part]}


LOW_AT, HIGH_AT = places(Y_LOW), places(Y_HIGH)


def node_rows(refs, table, sizes, f, c, x):
    part, at, n = table[c, x]
    return refs[part][pl.ds(f * sizes[part] + at, n), :]


def zone_rows(refs, sizes, i, which):
    part = 0 if 0 <= i < MX else 1
    k = i if part == 0 else (i + 2 if i < 0 else i - MX + 2)
    return refs[part][pl.ds(2 * sizes[part] + 2 * k, 2), which * MZ : (which + 1) * MZ]


def zone_block(zones, pressure, rho, low, high, ylow, yhigh):
    for which in range(2):
        for i in range(-2, MX + 2):
            k = which * (MX + 4) + i + 2
            zones[k, pl.ds(4, MY), :MZ] = zone_plane(i, (pressure, rho), low, high, which)
            zones[k, pl.ds(2, 2), :MZ] = zone_rows(ylow, Y_LOW_N, i, which)
            zones[k, pl.ds(4 + MY, 2), :MZ] = zone_rows(yhigh, Y_HIGH_N, i, which)


def third_kernel(
    d, v, low, high, pressure, rho, tracer, ylow_near, ylow_far, yhigh_near, yhigh_far,
    zlow, zhigh, zones, lefts, rights,
):
    ylow, yhigh = (ylow_near, ylow_far), (yhigh_near, yhigh_far)
    zone_block(zones, pressure, rho, low, high, ylow, yhigh)
    lane = lax.broadcasted_iota(jnp.int32, (1, 128), 1)
    for tile in range(Z_TILES):
        zlow[tile] = jnp.zeros((48, 128), F32)
        zhigh[tile] = jnp.zeros((48, 128), F32)
    for slot in range(TRACER_SLOT + MX):
        tile, s = divmod(slot, 32)
        here = (lane >= 4 * s) & (lane < 4 * s + 4)

        def put(rows, left, right):
            zhigh[tile, rows] = jnp.where(here, roll(left, 4 * s, 1), zhigh[tile, rows])
            zlow[tile, rows] = jnp.where(here, roll(right, 4 * s + 4, 1), zlow[tile, rows])

        if slot < ZONE_SLOT:
            f, e = divmod(slot, ZN)
            c, x = Z_PLANES[e]
            plane = node_pair(c, x, d, v, low, high)[f]
            put(pl.ds(8, NY), plane[:, :128], plane[:, 128:])
            if (c, x) in LOW_AT:
                n = LOW_AT[c, x][2]
                lefts[pl.ds(8 - n, n), :] = node_rows(ylow, LOW_AT, Y_LOW_N, f, c, x)
                put(pl.ds(0, 8), lefts[:, :128], lefts[:, 128:])
            if (c, x) in HIGH_AT:
                n = HIGH_AT[c, x][2]
                rights[pl.ds(0, n), :] = node_rows(yhigh, HIGH_AT, Y_HIGH_N, f, c, x)
                put(pl.ds(8 + NY, 8), rights[:, :128], rights[:, 128:])
        elif slot < TRACER_SLOT:
            put(pl.ds(0, 24), zones[slot - ZONE_SLOT], zones[slot - ZONE_SLOT])
        else:
            put(pl.ds(0, MY), tracer[slot - TRACER_SLOT], tracer[slot - TRACER_SLOT])


def roll(value, by, axis):
    by %= value.shape[axis]
    return pltpu.roll(value, by, axis) if by else value


def pieces(value):
    first = value.astype(jnp.bfloat16)
    rest = value - first.astype(F32)
    second = rest.astype(jnp.bfloat16)
    return first, second, (rest - second.astype(F32)).astype(jnp.bfloat16)


def product(parts, matrix):
    total = None
    for part in parts:
        term = jnp.dot(part, matrix, preferred_element_type=F32)
        total = term if total is None else total + term
    return total


def last_kernel(
    r, d, v, low, high, pressure, rho, tracer, ylow_near, ylow_far, yhigh_near, yhigh_far,
    zlow, zhigh,
    velocity, relaxed, remapped,
    moved, once, pz, qx, qy, qz, qm, moves, gathered, result, tz,
):
    ylow, yhigh = (ylow_near, ylow_far), (yhigh_near, yhigh_far)
    step = step_of(r)
    lane = lax.broadcasted_iota(jnp.int32, (1, 128), 1)

    def beside(slot, n, fill):
        tile, s = divmod(slot, 32)
        rows = pl.ds(0, n)
        after = roll(zhigh[tile, rows], -4 * s, 1)
        before = roll(zlow[tile, rows], 124 - 4 * s, 1)
        return jnp.where(lane < 4, after, jnp.where(lane >= 124, before, fill))

    zone_block(pz, pressure, rho, low, high, ylow, yhigh)
    for k in range(2 * (MX + 4)):
        pz[k, :, MZ:] = beside(ZONE_SLOT + k, 24, 0.0 if k < MX + 4 else 1.0)
    k = lax.broadcasted_iota(jnp.int32, (2 * MZ, 384), 0)
    n = lax.broadcasted_iota(jnp.int32, (2 * MZ, 384), 1)
    a = jnp.where(n < 320, n, n - 384) - 2 * jnp.where(k < 192, k, k - 256)
    shape = jnp.where((a == 0) | (a == 2), 1.0, jnp.where(a == 1, 4.0, 0.0)).astype(jnp.bfloat16)
    slope = jnp.where(a == 0, -1.0, jnp.where(a == 2, 1.0, 0.0)).astype(jnp.bfloat16)
    half = (MX + 4) * 24
    both = pz[...].reshape(2 * half, 2 * MZ)
    spread = product(pieces(both), shape)
    slanted = product(pieces(both[:half]), slope)
    even, odd = pl.ds(0, 24, stride=2), pl.ds(1, 24, stride=2)

    def interleave(q, i, first, second):
        for t in range(3):
            lanes = slice(128 * t, 128 * t + 128)
            q[3 * i + t, even, :] = first[:, lanes]
            q[3 * i + t, odd, :] = second[:, lanes]

    def whole(q, i):
        return jnp.concatenate([q[3 * i + t] for t in range(3)], axis=1)

    for i in range(MX + 4):
        now = spread[24 * i : 24 * i + 24]
        before = roll(now, 1, 0)
        interleave(qx, i, now + before, 4.0 * now)
        interleave(qy, i, before - now, jnp.zeros((24, 384), F32))
        now = slanted[24 * i : 24 * i + 24]
        interleave(qz, i, now + roll(now, 1, 0), 4.0 * now)
        now = spread[half + 24 * i : half + 24 * i + 24]
        interleave(qm, i, now + roll(now, 1, 0), 4.0 * now)
    for x in range(-3, NX + 4):
        i = x // 2 + 2
        mass = whole(qm, i)
        mass = mass + whole(qm, i - 1) if x % 2 == 0 else 4.0 * mass
        push = 6.0 * step / mass
        for c in range(3):
            if (c, x) not in PLANE_AT:
                continue
            e = PLANE_AT[c, x]
            if c == 0:
                force = whole(qx, i - 1) - whole(qx, i) if x % 2 == 0 else None
            else:
                q = qy if c == 1 else qz
                force = whole(q, i)
                force = force + whole(q, i - 1) if x % 2 == 0 else 4.0 * force
            here, there = node_pair(c, x, d, v, low, high)
            moved[e, pl.ds(8, NY), :NZ] = here[...] + step * there[...]
            if (c, x) in LOW_AT:
                n = LOW_AT[c, x][2]
                here, there = (node_rows(ylow, LOW_AT, Y_LOW_N, f, c, x) for f in range(2))
                moved[e, pl.ds(8 - n, n), :NZ] = here + step * there
            if (c, x) in HIGH_AT:
                n = HIGH_AT[c, x][2]
                here, there = (node_rows(yhigh, HIGH_AT, Y_HIGH_N, f, c, x) for f in range(2))
                moved[e, pl.ds(8 + NY, n), :NZ] = here + step * there
            if (c, x) in Z_PLANES:
                z = Z_PLANES.index((c, x))
                moved[e, :, NZ:] = beside(z, 48, 0.0) + step * beside(ZN + z, 48, 0.0)
            else:
                moved[e, :, NZ:] = jnp.zeros((48, 128), F32)
            if force is not None:
                gain = force * push
                moved[e] = moved[e] + step * gain
            if 0 <= x < NX:
                new = v[c, x]
                velocity[c, x] = new if force is None else new + gain[8 : 8 + NY, :NZ]

    def sweep(ref, e, first, count, width):
        rows = pl.ds(first, count)
        now = ref[e, rows]
        sides = roll(now, 1, 1) + roll(now, -1, 1)
        rows_beside = ref[e, pl.ds(first - 1, count), :width] + ref[e, pl.ds(first + 1, count), :width]
        planes_beside = ref[e - 1, rows, :width] + ref[e + 1, rows, :width]
        total = planes_beside + rows_beside + sides[:, :width]
        return 0.1 * now[:, :width] + 0.15 * total

    for e, (c, x) in enumerate(PLANES):
        if (c, x - 1) in PLANE_AT and (c, x + 1) in PLANE_AT:
            now = moved[e]
            total = moved[e - 1] + moved[e + 1]
            total = total + (roll(now, 1, 0) + roll(now, -1, 0))
            total = total + (roll(now, 1, 1) + roll(now, -1, 1))
            once[e] = 0.1 * now + 0.15 * total
    at = 0
    for e, (c, x) in enumerate(PLANES):
        inside = 0 <= x < NX
        if not inside and not (c == 0 and x in (-1, NX + 1)):
            continue
        width = 384 if c == 2 and x % 2 else NZ
        if c == 1 and x % 2:
            edges = (sweep(once, e, 7, 1, width), sweep(once, e, 41, 1, width))
        twice = sweep(once, e, 8, NY, width)
        if inside:
            relaxed[c, x] = twice[:, :NZ]
        if x % 2:
            first, count = (7, 18) if c == 1 else (9, 16)
            for t in range(width // 128):
                lanes = slice(128 * t, 128 * t + 128)
                moves[t, pl.ds(8, NY), :] = twice[:, lanes] - moved[e, pl.ds(8, NY), lanes]
                if c == 1:
                    for row, edge in zip((7, 41), edges):
                        moves[t, pl.ds(row, 1), :] = edge[:, lanes] - moved[e, pl.ds(row, 1), lanes]
                gathered[pl.ds(at, count), lanes] = moves[t, pl.ds(first, count, stride=2), :]
            if c == 1:
                gathered[pl.ds(at + 18, 6), :] = jnp.zeros((6, 384), F32)
            at += 24 if c == 1 else 16
    gathered[pl.ds(0, (MX + 2) * 16 + MX * 24), NZ:] = jnp.zeros(((MX + 2) * 16 + MX * 24, 128), F32)
    n = lax.broadcasted_iota(jnp.int32, (384, 2 * MZ), 0)
    k = lax.broadcasted_iota(jnp.int32, (384, 2 * MZ), 1)
    node = jnp.where(n < 320, n, n - 384)
    chosen = (node == 2 * jnp.where(k < 192, k, k - 256) + 1).astype(F32).astype(jnp.bfloat16)
    result[...] = product(pieces(gathered[...]), chosen)

    def flux(speed, behind, here):
        donor = -(jnp.minimum(speed, 0.0) * behind + jnp.maximum(speed, 0.0) * here)
        return donor, -speed * 0.5 * (behind + here)

    y0, z0 = (MX + 2) * 16, (MX + 2) * 16 + MX * 24
    for i in range(MX):
        now = tracer[i]
        tz[pl.ds(8, MY), :] = now
        tz[pl.ds(7, 1), :] = ylow_near[pl.ds(2 * Y_LOW_N[0] + 2 * MX + i, 1), :MZ]
        tz[pl.ds(8 + MY, 1), :] = yhigh_near[pl.ds(2 * Y_HIGH_N[0] + 2 * MX + i, 1), :MZ]
        side = beside(TRACER_SLOT + i, MY, 0.0)
        edge = result[pl.ds(z0 + 16 * i, 16), MZ:]
        middle = result[pl.ds(z0 + 16 * i, 16), :MZ]
        around = (
            (
                tracer[i - 1] if i else low[2 * NL + 1, :MY, :MZ],
                tracer[i + 1] if i < MX - 1 else high[2 * NH + 1, :MY, :MZ],
                result[pl.ds(16 * i, 16), :MZ],
                result[pl.ds(16 * (i + 1), 16), :MZ],
                result[pl.ds(16 * (i + 2), 16), :MZ],
            ),
            (
                tz[pl.ds(7, MY), :],
                tz[pl.ds(9, MY), :],
                result[pl.ds(y0 + 24 * i, 16), :MZ],
                result[pl.ds(y0 + 24 * i + 1, 16), :MZ],
                result[pl.ds(y0 + 24 * i + 2, 16), :MZ],
            ),
            (
                jnp.where(lane == 0, roll(side, 1, 1), roll(now, 1, 1)),
                jnp.where(lane == MZ - 1, roll(side, -1, 1), roll(now, -1, 1)),
                jnp.where(lane == 0, roll(edge, 1, 1), roll(middle, 1, 1)),
                middle,
                jnp.where(lane == MZ - 1, roll(edge, -1, 1), roll(middle, -1, 1)),
            ),
        )
        donors = centrals = None
        floor = ceiling = now
        for behind, front, m0, m1, m2 in around:
            d0, c0 = flux(0.5 * (m0 + m1), behind, now)
            d1, c1 = flux(0.5 * (m1 + m2), now, front)
            donors = d1 - d0 if donors is None else donors + (d1 - d0)
            centrals = c1 - c0 if centrals is None else centrals + (c1 - c0)
            floor = jnp.minimum(jnp.minimum(floor, behind), front)
            ceiling = jnp.maximum(jnp.maximum(ceiling, behind), front)
        low_order = now - donors
        high_order = now - centrals
        floor = jnp.minimum(floor, low_order)
        ceiling = jnp.maximum(ceiling, low_order)
        remapped[i] = jnp.minimum(jnp.maximum(high_order, floor), ceiling)


def shape_of(*dims):
    return jax.ShapeDtypeStruct(dims, F32)


def local_of(*dims):
    return pltpu.VMEM(dims, F32)


def on_chip(array):
    return pltpu.with_memory_space_constraint(array, pltpu.VMEM)


def in_hbm(array):
    return pltpu.with_memory_space_constraint(array, pltpu.HBM)


def moved_along(block, axis, by):
    n = lax.axis_size(axis)
    return on_chip(lax.ppermute(block, axis, [(i, (i + by) % n) for i in range(n)]))


def pack_y(*operands):
    return pl.pallas_call(
        second_kernel,
        name="second",
        compiler_params=pltpu.CompilerParams(vmem_limit_bytes=8 << 20),
        in_specs=[VM] * 2,
        out_specs=[VM] * 2,
        out_shape=[local_of(buffer_rows(n, 1), NZ) for n in (Y_LOW_N, Y_HIGH_N)],
    )(*operands)


def on_device(displacement, velocity, density, energy, region, heat_ratio, tracer):
    n_devices = lax.axis_size(AXES)
    low, high, most, pressure, density, tracer, near_low, near_high = pl.pallas_call(
        first_kernel,
        name="first",
        compiler_params=pltpu.CompilerParams(vmem_limit_bytes=8 << 20),
        in_specs=[SM] + [HB] * 6,
        out_specs=[VM] * 8,
        out_shape=[
            local_of(2 * NL + 2, NY, NZ),
            local_of(2 * NH + 2, NY, NZ),
            local_of(n_devices, 128),
            local_of(MX, MY, MZ),
            local_of(MX, MY, MZ),
            local_of(MX, MY, MZ),
            local_of(buffer_rows(Y_LOW_N, 0), NZ),
            local_of(buffer_rows(Y_HIGH_N, 0), NZ),
        ],
        scratch_shapes=[
            pltpu.VMEM((MX, MY, MZ), F32),
            pltpu.VMEM((MX, MY, MZ), jnp.int32),
            pltpu.VMEM((2, 3, NX, 8, NZ), F32),
            pltpu.VMEM((2, 3, NX, 8, NZ), F32),
            pltpu.SemaphoreType.DMA((20,)),
        ],
    )(*map(in_hbm, (heat_ratio, displacement, velocity, density, energy, region, tracer)))
    displacement, velocity = on_chip(displacement), on_chip(velocity)
    low = moved_along(low, "gx", 1)
    high = moved_along(high, "gx", -1)
    near_low = moved_along(near_low, "gy", 1)
    near_high = moved_along(near_high, "gy", -1)
    r = on_chip(lax.all_to_all(most, AXES, 0, 0, tiled=True))
    far_low, far_high = pack_y(low, high)
    far_low = moved_along(far_low, "gy", 1)
    far_high = moved_along(far_high, "gy", -1)
    halo = (near_low, far_low, near_high, far_high)
    zlow, zhigh = pl.pallas_call(
        third_kernel,
        name="third",
        compiler_params=pltpu.CompilerParams(vmem_limit_bytes=8 << 20),
        in_specs=[VM] * 11,
        out_specs=[VM] * 2,
        out_shape=[local_of(Z_TILES, 48, 128)] * 2,
        scratch_shapes=[
            pltpu.VMEM((2 * (MX + 4), 24, MZ), F32),
            pltpu.VMEM((8, NZ), F32),
            pltpu.VMEM((8, NZ), F32),
        ],
    )(displacement, velocity, low, high, pressure, density, tracer, *halo)
    zlow = moved_along(zlow, "gz", 1)
    zhigh = moved_along(zhigh, "gz", -1)
    q = pltpu.VMEM((3 * (MX + 4), 48, 128), F32)
    return pl.pallas_call(
        last_kernel,
        name="last",
        compiler_params=pltpu.CompilerParams(vmem_limit_bytes=30 << 20),
        in_specs=[VM] * 14,
        out_specs=[VM] * 3,
        out_shape=[shape_of(3, NX, NY, NZ), shape_of(3, NX, NY, NZ), shape_of(MX, MY, MZ)],
        scratch_shapes=[
            pltpu.VMEM((NP, 48, 384), F32),
            pltpu.VMEM((NP, 48, 384), F32),
            pltpu.VMEM((2 * (MX + 4), 24, 2 * MZ), F32),
            q, q, q, q,
            pltpu.VMEM((3, 48, 128), F32),
            pltpu.VMEM((256, 384), F32),
            pltpu.VMEM((256, 2 * MZ), F32),
            pltpu.VMEM((MY + 16, MZ), F32),
        ],
    )(
        r, displacement, velocity, low, high, pressure, density, tracer, *halo, zlow, zhigh
    )


def solution(mesh):
    node, zone = P(None, "gx", "gy", "gz"), P("gx", "gy", "gz")
    return jax.shard_map(
        on_device,
        mesh=mesh,
        in_specs=(node, node, zone, zone, zone, P(), zone),
        out_specs=(node, node, zone),
        check_vma=False,
    )
```
